1024 devices in a mesh: space: 16 (over y_lo, z), batch: 64 (over x, y_hi, core).
Axes of the slice: x: 8, y: 8 (y_hi: 4, y_lo: 2; y = y_hi * 2 + y_lo), z: 8, core: 2. Of those that a mesh axis runs over, the one named last changes fastest.
Arguments:
- volume: bfloat16 [64, 4, 128, 32, 128], P('batch', None, 'space'), may hold values from -6 to 6
- kernel: bfloat16 [32, 108], replicated, may hold values from -0.625 to 0.625
- bias: float32 [32], replicated, may hold values from -3 to 3
- cotangent: bfloat16 [64, 32, 64, 1024], P('batch', 'space'), may hold values from -0.062148057 to 0.062148057
Outputs:
- pooled: bfloat16 [64, 32, 64, 1024], P('batch', 'space')
- kernel_grad: float32 [32, 108], replicated
- bias_grad: float32 [32], replicated
The draws below stay inside these ranges and needn't reach their ends.
All inputs are finite; a program needn't handle non-finite values.
Results may differ from the reference program's by a relative error of at most 0.0065.
Values may be sent and summed in bfloat16 or wider, within the bound.
No kernel may reach another device: no remote copies, remote signals or barrier semaphores. Data moves between devices by JAX's collectives and lax.ppermute only.
A program may use at most 32 MiB of HBM per device.

```python
import jax
import jax.numpy as jnp
from jax import lax

CIN = 4
C1 = 32
HEIGHT = 32
WIDTH = 128
SAMPLES = 64
DEPTH = 128
PDEPTH = 64
PPLANE = 1024


def draw_cotangent(key, part):
    shape = (SAMPLES, C1, PDEPTH, PPLANE)
    sample_rise = 10.0 ** (jnp.arange(SAMPLES, dtype=jnp.float32) / max(SAMPLES - 1, 1))
    depth_rise = 3.0 ** (jnp.arange(PDEPTH, dtype=jnp.float32) / max(PDEPTH - 1, 1))
    factor = sample_rise[:, None, None, None] * depth_rise[None, None, :, None]
    scale = 2.0 / (8.0 * SAMPLES * PDEPTH * PPLANE) ** 0.5
    base = jnp.clip(jax.random.normal(key, shape, jnp.float32), -6.0, 6.0)
    return (base * factor * scale).astype(jnp.bfloat16)


def block_levels(stream_key, shape, split, least, largest):
    loudness, own = 1.0, jax.random.fold_in(stream_key, 6)
    for dim, shards_of in split:
        heights = jnp.exp(jax.random.uniform(jax.random.fold_in(own, dim), (shards_of,), jnp.float32, least / len(split), largest / len(split)))
        loudness = loudness * jnp.repeat(heights, shape[dim] // shards_of).reshape([-1 if axis == dim else 1 for axis in range(len(shape))])
    return loudness


def bell_draw(stream_key, shape, deviation, most, shards=(), kind=jnp.bfloat16):
    gain = block_levels(stream_key, shape, shards, -0.22, 0.18) if shards else 1.0
    entries = jax.random.normal(stream_key, shape, jnp.float32) * deviation * gain
    return jnp.minimum(jnp.maximum(entries, -most), most).astype(kind)


def setup_inputs(seed: int = 0) -> dict:
    key_of = jax.random.split(jax.random.key(seed), 5)
    return {
        "volume": bell_draw(key_of[0], (SAMPLES, CIN, DEPTH, HEIGHT, WIDTH), 1.0, 6.0, ((0, 64), (2, 16))),
        "kernel": bell_draw(key_of[1], (C1, 27 * CIN), (27 * CIN) ** -0.5, 0.625),
        "bias": bell_draw(key_of[2], (C1,), 0.5, 3.0, (), jnp.float32),
        "cotangent": draw_cotangent(jax.random.fold_in(key_of[4], 71), 0),
    }


def reference(volume, kernel, bias, cotangent):
    filters = kernel.astype(jnp.float32).reshape(C1, 3, 3, 3, CIN).transpose(0, 4, 1, 2, 3)

    def one_sample(pair):
        sample_volume, sample_cot = pair
        as_float = sample_volume.astype(jnp.float32)
        conv_out = lax.conv_general_dilated(as_float[None], filters, (1, 1, 1), ((1, 1), (1, 1), (1, 1)),
                                            dimension_numbers=("NCDHW", "OIDHW", "NCDHW"),
                                            precision=lax.Precision.HIGHEST)[0]
        conv_out = conv_out + bias[:, None, None, None]
        positive = conv_out > 0
        activated = jnp.where(positive, conv_out, 0.3 * conv_out).astype(jnp.bfloat16)
        pooled = activated.astype(jnp.float32).reshape(C1, DEPTH // 2, 2, HEIGHT // 2, 2, WIDTH // 2, 2)
        pooled = pooled.mean(axis=(2, 4, 6)).astype(jnp.bfloat16).reshape(C1, DEPTH // 2, PPLANE)
        incoming = sample_cot.astype(jnp.float32).reshape(C1, DEPTH // 2, 1, HEIGHT // 2, 1, WIDTH // 2, 1) * 0.125
        widened = jnp.broadcast_to(incoming, (C1, DEPTH // 2, 2, HEIGHT // 2, 2, WIDTH // 2, 2)).reshape(C1, DEPTH, HEIGHT, WIDTH)
        spread = (widened * jnp.where(positive, 1.0, 0.3)).astype(jnp.bfloat16).astype(jnp.float32)
        padded = jnp.pad(as_float, ((0, 0), (1, 1), (1, 1), (1, 1)))
        pieces = []
        for shift_d in range(3):
            for shift_h in range(3):
                for shift_w in range(3):
                    shifted = padded[:, shift_d:shift_d + DEPTH, shift_h:shift_h + HEIGHT, shift_w:shift_w + WIDTH]
                    pieces.append(jnp.einsum("odhw,cdhw->oc", spread, shifted, precision=lax.Precision.HIGHEST))
        kernel_part = jnp.stack(pieces, axis=1).reshape(C1, 27 * CIN)
        return pooled, kernel_part, jnp.sum(spread, axis=(1, 2, 3))

    pooled, kernel_parts, bias_parts = lax.map(one_sample, (volume, cotangent))
    return pooled, jnp.sum(kernel_parts, axis=0), jnp.sum(bias_parts, axis=0)
```

```python
import jax
import jax.numpy as jnp
import numpy as np
from jax import lax
from jax.experimental import pallas as pl
from jax.experimental.pallas import tpu as pltpu
from jax.sharding import PartitionSpec as P

CLASSES = [(pd, ph, pw) for pd in range(2) for ph in range(2) for pw in range(2)]
CHANNELS = 4
FILTERS = 32
TAPS = 27 * CHANNELS
ROWS = 48


def window_shift(pd, ph, pw):
    return ph * 64 + pw * 16 + pd * 4


def tap_table():
    table = np.zeros((128, 256), np.float32)
    for a in range(3):
        for b in range(3):
            for e in range(3):
                for c in range(CHANNELS):
                    table[(a * 9 + b * 3 + e) * CHANNELS + c, b * 64 + e * 16 + a * 4 + c] = 1.0
    return table


def width_table():
    table = np.zeros((2, 128, 4, 2, 64), np.float32)
    for half in range(2):
        for k in range(4):
            for cell in range(64):
                w = 2 * cell - 1 + k
                if 0 <= w < 128:
                    table[half, w, k, half, cell] = 1.0
    return table.reshape(256, 512)


def row_table(order):
    table = np.zeros((128, 128), np.float32)
    table[np.arange(128), order] = 1.0
    return table


def slab_kernel(
    vol_ref, low_ref, high_ref, kern_ref, bias_ref, cot_ref, taps_ref, width_ref, order_ref, back_ref,
    out_ref, flat, lines, split, window, spread, pooled, cots
):
    f32, bf16 = jnp.float32, jnp.bfloat16
    for c in range(CHANNELS):
        for d in range(10):
            if d == 0:
                plane = low_ref[c, 0]
            elif d == 9:
                plane = high_ref[c, 0]
            else:
                plane = vol_ref[c, d - 1]
            flat[(d * CHANNELS + c) * 32 : (d * CHANNELS + c + 1) * 32, :] = plane.astype(f32)
    zero_line = jnp.zeros((ROWS, 128), bf16)
    lines[0, :, 0:128] = zero_line
    lines[31, :, 128:256] = zero_line
    for h in range(32):
        line = flat[pl.ds(h, 40, stride=32), :]
        line = jnp.concatenate([line, jnp.zeros((8, 128), f32)], axis=0).astype(bf16)
        if h <= 30:
            h4, j = divmod(h + 1, 4)
            lines[j * 8 + h4, :, 0:128] = line
        if h >= 1:
            h4, j = divmod(h - 1, 4)
            lines[j * 8 + h4, :, 128:256] = line
    for j in range(4):
        rows = lines[j * 8 : (j + 1) * 8].reshape(8 * ROWS, 256)
        split[j] = jnp.dot(rows, width_ref[...], preferred_element_type=f32)
    for d2 in range(4):
        for h4 in range(8):
            for j in range(4):
                for k in range(4):
                    first = h4 * ROWS + d2 * 8
                    window[
                        (j * 4 + k) * 16 : (j * 4 + k + 1) * 16,
                        (d2 * 8 + h4) * 128 : (d2 * 8 + h4 + 1) * 128,
                    ] = split[j, first : first + 16, k * 128 : (k + 1) * 128].astype(bf16)

    spread_taps = jnp.dot(kern_ref[...], taps_ref[...], preferred_element_type=f32)
    weights = jnp.concatenate(
        [
            pltpu.roll(spread_taps, window_shift(*parity), 1) if window_shift(*parity) else spread_taps
            for parity in CLASSES
        ],
        axis=0,
    ).astype(bf16)

    cots[...] = jnp.dot(order_ref[...], cot_ref[...], preferred_element_type=f32)
    bias = jnp.broadcast_to(bias_ref[...], (FILTERS, 128))
    bias_sum = jnp.zeros((FILTERS, 128), f32)
    for d2 in range(4):
        for tile in range(4):
            first = d2 * 1024 + tile * 256
            conv = jnp.dot(weights, window[:, first : first + 256], preferred_element_type=f32)
            for half in range(2):
                lane = tile * 256 + half * 128
                incoming = cots[d2 * FILTERS : (d2 + 1) * FILTERS, lane : lane + 128] * 0.125
                full = incoming.astype(bf16).astype(f32)
                part = (incoming * 0.3).astype(bf16).astype(f32)
                total = jnp.zeros((FILTERS, 128), f32)
                for n in range(8):
                    x = conv[n * FILTERS : (n + 1) * FILTERS, half * 128 : (half + 1) * 128] + bias
                    total = total + jnp.maximum(x, 0.3 * x).astype(bf16).astype(f32)
                    back = jnp.where(x > 0, full, part)
                    bias_sum = bias_sum + back
                    spread[
                        n * FILTERS : (n + 1) * FILTERS,
                        first + half * 128 : first + (half + 1) * 128,
                    ] = back.astype(bf16)
                pooled[d2 * FILTERS : (d2 + 1) * FILTERS, lane : lane + 128] = (total * 0.125).astype(bf16)

    out_ref[:, 0:1024] = jnp.dot(back_ref[...], pooled[...], preferred_element_type=f32).astype(bf16)

    grads = lax.dot_general(
        spread[...], window[...], (((1,), (1,)), ((), ())), preferred_element_type=f32
    )
    folded = jnp.zeros((FILTERS, 256), f32)
    for n, parity in enumerate(CLASSES):
        shift = window_shift(*parity)
        block = grads[n * FILTERS : (n + 1) * FILTERS]
        folded = folded + (pltpu.roll(block, 256 - shift, 1) if shift else block)

    def pieces(value):
        one = value.astype(bf16)
        rest = value - one.astype(f32)
        two = rest.astype(bf16)
        three = (rest - two.astype(f32)).astype(bf16)
        return one, two, three

    bias_column = jnp.sum(bias_sum, axis=1, keepdims=True)
    columns = lax.broadcasted_iota(jnp.int32, (FILTERS, 128), 1)
    sent = []
    for taps, own in zip(pieces(folded), pieces(bias_column), strict=True):
        picked = lax.dot_general(taps, taps_ref[...], (((1,), (1,)), ((), ())), preferred_element_type=f32)
        sent.append(jnp.where(columns == TAPS, own.astype(f32), picked))
    sent.append(jnp.zeros((FILTERS, 128), f32))
    stacked = jnp.concatenate(sent, axis=0).astype(bf16)
    out_ref[:, 1024:1152] = jnp.dot(back_ref[...], stacked, preferred_element_type=f32).astype(bf16)


def slab(volume, low, high, kernel, bias, cots):
    f32, bf16 = jnp.float32, jnp.bfloat16
    by_depth = np.array([o * 4 + d for d in range(4) for o in range(FILTERS)])
    by_filter = np.argsort(by_depth)
    taps = jnp.asarray(tap_table(), bf16)
    width = jnp.asarray(width_table(), bf16)
    order = jnp.asarray(row_table(by_depth), bf16)
    back = jnp.asarray(row_table(by_filter), bf16)
    padded = jnp.pad(kernel, ((0, 0), (0, 128 - TAPS)))
    operands = (volume, low, high, padded, bias[:, None], cots, taps, width, order, back)
    return pl.pallas_call(
        slab_kernel,
        out_shape=jax.ShapeDtypeStruct((128, 1152), bf16),
        in_specs=[pl.BlockSpec(memory_space=pltpu.VMEM)] * len(operands),
        out_specs=pl.BlockSpec(memory_space=pltpu.VMEM),
        scratch_shapes=[
            pltpu.VMEM((1280, 128), f32),
            pltpu.VMEM((32, ROWS, 256), bf16),
            pltpu.VMEM((4, 8 * ROWS, 512), f32),
            pltpu.VMEM((256, 4096), bf16),
            pltpu.VMEM((256, 4096), bf16),
            pltpu.VMEM((128, 1024), bf16),
            pltpu.VMEM((128, 1024), f32),
        ],
        compiler_params=pltpu.CompilerParams(vmem_limit_bytes=24 * 1024 * 1024),
        cost_estimate=pl.CostEstimate(flops=1_500_000_000, bytes_accessed=2_000_000, transcendentals=0),
    )(*operands)


def reorder(order, rows):
    return jnp.dot(jnp.asarray(row_table(order), rows.dtype), rows, preferred_element_type=rows.dtype)


def on_device(volume, kernel, bias, cotangent):
    f32 = jnp.float32
    spaces, batches = lax.axis_size("space"), lax.axis_size("batch")
    owned_rows = np.arange(128).reshape(2, spaces, 4)
    to_slabs = owned_rows.transpose(1, 0, 2).reshape(-1)
    to_owner = np.argsort(to_slabs)

    up = [(i, i + 1) for i in range(spaces - 1)]
    down = [(i + 1, i) for i in range(spaces - 1)]
    local = volume[0]
    sent = reorder(to_slabs, cotangent.reshape(128, 1024))
    low = lax.ppermute(local[:, -1:], "space", up)
    high = lax.ppermute(local[:, :1], "space", down)
    cots = lax.all_to_all(sent, "space", split_axis=0, concat_axis=0, tiled=True)

    out = slab(local, low, high, kernel, bias, cots)

    out = lax.all_to_all(out, "space", split_axis=0, concat_axis=0, tiled=True)
    pooled = reorder(to_owner, out[:, :1024]).reshape(1, 2, 64, 1024)
    terms = jnp.sum(out[:, 1024:].reshape(spaces, 2, 4, 128).astype(f32), axis=(0, 2))
    terms = lax.all_to_all(
        jnp.broadcast_to(terms[None], (batches, 2, 128)), "batch", split_axis=0, concat_axis=0, tiled=True
    )
    terms = jnp.sum(terms, axis=0)
    terms = lax.all_to_all(
        jnp.broadcast_to(terms[None], (spaces, 2, 128)), "space", split_axis=0, concat_axis=0, tiled=True
    ).reshape(FILTERS, 128)
    return (pooled, terms[:, :TAPS], terms[:, TAPS])


def solution(mesh):
    placed = (P("batch", None, "space", None, None), P(), P(), P("batch", "space", None, None))
    return jax.shard_map(
        on_device,
        mesh=mesh,
        in_specs=placed,
        out_specs=(P("batch", "space", None, None), P(), P()),
        check_vma=False,
    )
```

```python
import jax
import jax.numpy as jnp
import numpy as np
from jax import lax
from jax.experimental import pallas as pl
from jax.experimental.pallas import tpu as pltpu
from jax.sharding import PartitionSpec as P


CLASSES = [(pd, ph, pw) for pd in range(2) for ph in range(2) for pw in range(2)]
CHANNELS = 4
FILTERS = 32
TAPS = 27 * CHANNELS
ROWS = 48


def window_shift(pd, ph, pw):
    return ph * 64 + pw * 16 + pd * 4


def tap_table():
    tap = lax.broadcasted_iota(jnp.int32, (128, 256), 0)
    row = lax.broadcasted_iota(jnp.int32, (128, 256), 1)
    j, k, i, c = row >> 6, (row >> 4) & 3, (row >> 2) & 3, row & 3
    inside = (i < 3) & (j < 3) & (k < 3)
    return jnp.where(inside & (tap == (i * 9 + j * 3 + k) * CHANNELS + c), 1.0, 0.0).astype(jnp.bfloat16)


def width_table():
    row = lax.broadcasted_iota(jnp.int32, (256, 512), 0)
    col = lax.broadcasted_iota(jnp.int32, (256, 512), 1)
    same = (row >> 7) == ((col >> 6) & 1)
    return jnp.where(same & ((row & 127) == 2 * (col & 63) - 1 + (col >> 7)), 1.0, 0.0).astype(jnp.bfloat16)


def depth_table(inverse):
    row = lax.broadcasted_iota(jnp.int32, (128, 128), 0)
    col = lax.broadcasted_iota(jnp.int32, (128, 128), 1)
    if inverse:
        row, col = col, row
    return jnp.where(col == (row & 31) * 4 + (row >> 5), 1.0, 0.0).astype(jnp.bfloat16)


def row_table(order):
    table = np.zeros((128, 128), np.float32)
    table[np.arange(128), order] = 1.0
    return table


def forward_kernel(
    vol_ref, low_ref, high_ref, kern_ref, bias_ref, pooled_ref, window, code_ref,
    flat, lines, split, pooled, width
):
    f32, bf16 = jnp.float32, jnp.bfloat16
    width[...] = width_table()
    spread_taps = jnp.dot(kern_ref[...], tap_table(), preferred_element_type=f32)
    weights = jnp.concatenate(
        [
            pltpu.roll(spread_taps, window_shift(*parity), 1) if window_shift(*parity) else spread_taps
            for parity in CLASSES
        ],
        axis=0,
    ).astype(bf16)
    bias = bias_ref[...]
    for c in range(CHANNELS):
        for d in range(10):
            if d == 0:
                plane = low_ref[c, 0]
            elif d == 9:
                plane = high_ref[c, 0]
            else:
                plane = vol_ref[c, d]
            flat[(d * CHANNELS + c) * 32 : (d * CHANNELS + c + 1) * 32, :] = plane.astype(f32)
    zero_line = jnp.zeros((ROWS, 128), bf16)
    lines[0, :, 0:128] = zero_line
    lines[31, :, 128:256] = zero_line
    for h in range(32):
        line = flat[pl.ds(h, 40, stride=32), :]
        line = jnp.concatenate([line, jnp.zeros((8, 128), f32)], axis=0).astype(bf16)
        if h <= 30:
            h4, j = divmod(h + 1, 4)
            lines[j * 8 + h4, :, 0:128] = line
        if h >= 1:
            h4, j = divmod(h - 1, 4)
            lines[j * 8 + h4, :, 128:256] = line
    for j in range(4):
        rows = lines[j * 8 : (j + 1) * 8].reshape(8 * ROWS, 256)
        split[j] = jnp.dot(rows, width[...], preferred_element_type=f32)
    for d2 in range(4):
        for h4 in range(8):
            for j in range(4):
                for k in range(4):
                    first = h4 * ROWS + d2 * 8
                    window[
                        (j * 4 + k) * 16 : (j * 4 + k + 1) * 16,
                        (d2 * 8 + h4) * 128 : (d2 * 8 + h4 + 1) * 128,
                    ] = split[j, first : first + 16, k * 128 : (k + 1) * 128].astype(bf16)

    for d2 in range(4):
        for tile in range(4):
            first = d2 * 1024 + tile * 256
            conv = jnp.dot(weights, window[:, first : first + 256], preferred_element_type=f32)
            for half in range(2):
                lane = tile * 256 + half * 128
                total = jnp.zeros((FILTERS, 128), f32)
                code = jnp.zeros((FILTERS, 128), f32)
                for n in range(8):
                    x = conv[n * FILTERS : (n + 1) * FILTERS, half * 128 : (half + 1) * 128] + bias
                    total = total + jnp.maximum(x, 0.3 * x).astype(bf16).astype(f32)
                    code = code + jnp.where(x > 0, float(1 << n), 0.0)
                code_ref[d2 * FILTERS : (d2 + 1) * FILTERS, lane : lane + 128] = code.astype(bf16)
                pooled[d2 * FILTERS : (d2 + 1) * FILTERS, lane : lane + 128] = (total * 0.125).astype(bf16)
    pooled_ref[...] = jnp.dot(depth_table(True), pooled[...], preferred_element_type=f32).astype(bf16)


def backward_kernel(pooled_ref, window, code_ref, cot_ref, out_ref, spread, cots):
    f32, bf16 = jnp.float32, jnp.bfloat16
    out_ref[:, 0:1024] = pooled_ref[...]
    cots[...] = jnp.dot(depth_table(False), cot_ref[...], preferred_element_type=f32)
    bias_sum = jnp.zeros((FILTERS, 128), f32)
    for d2 in range(4):
        for tile in range(8):
            lane = tile * 128
            first = d2 * 1024 + lane
            incoming = cots[d2 * FILTERS : (d2 + 1) * FILTERS, lane : lane + 128] * 0.125
            full = incoming.astype(bf16).astype(f32)
            part = (incoming * 0.3).astype(bf16).astype(f32)
            code = code_ref[d2 * FILTERS : (d2 + 1) * FILTERS, lane : lane + 128].astype(f32).astype(jnp.int32)
            for n in range(8):
                back = jnp.where((code & (1 << n)) != 0, full, part)
                bias_sum = bias_sum + back
                spread[n * FILTERS : (n + 1) * FILTERS, first : first + 128] = back.astype(bf16)

    grads = lax.dot_general(
        spread[...], window[...], (((1,), (1,)), ((), ())), preferred_element_type=f32
    )
    table = tap_table()
    folded = jnp.zeros((FILTERS, 256), f32)
    for n, parity in enumerate(CLASSES):
        shift = window_shift(*parity)
        block = grads[n * FILTERS : (n + 1) * FILTERS]
        folded = folded + (pltpu.roll(block, 256 - shift, 1) if shift else block)

    def pieces(value):
        one = value.astype(bf16)
        rest = value - one.astype(f32)
        two = rest.astype(bf16)
        three = (rest - two.astype(f32)).astype(bf16)
        return one, two, three

    bias_column = jnp.sum(bias_sum, axis=1, keepdims=True)
    columns = lax.broadcasted_iota(jnp.int32, (FILTERS, 128), 1)
    sent = []
    for taps, own in zip(pieces(folded), pieces(bias_column), strict=True):
        picked = lax.dot_general(taps, table, (((1,), (1,)), ((), ())), preferred_element_type=f32)
        sent.append(jnp.where(columns == TAPS, own.astype(f32), picked))
    sent.append(jnp.zeros((FILTERS, 128), f32))
    stacked = jnp.concatenate(sent, axis=0).astype(bf16)
    out_ref[:, 1024:1152] = jnp.dot(depth_table(True), stacked, preferred_element_type=f32).astype(bf16)


def unpack_kernel(terms_ref, kernel_ref, bias_ref):
    terms = terms_ref[...]
    kernel_ref[...] = terms[:, :TAPS]
    own = lax.broadcasted_iota(jnp.int32, (FILTERS, FILTERS), 0) == lax.broadcasted_iota(
        jnp.int32, (FILTERS, FILTERS), 1
    )
    bias_ref[...] = jnp.sum(jnp.where(own, terms[:, TAPS : TAPS + 1], 0.0), axis=0, keepdims=True)


def in_vmem(kernel, outs, operands, scratch=(), megabytes=24, flops=1_000_000, moved=100_000):
    one = pl.BlockSpec(memory_space=pltpu.VMEM)
    return pl.pallas_call(
        kernel,
        out_shape=outs,
        in_specs=[one] * len(operands),
        out_specs=jax.tree.map(lambda _: one, outs),
        scratch_shapes=list(scratch),
        compiler_params=pltpu.CompilerParams(vmem_limit_bytes=megabytes * 1024 * 1024),
        cost_estimate=pl.CostEstimate(flops=flops, bytes_accessed=moved, transcendentals=0),
    )(*operands)


def reorder(order, rows):
    return jnp.dot(jnp.asarray(row_table(order), rows.dtype), rows, preferred_element_type=rows.dtype)


def on_device(volume, kernel, bias, cotangent):
    f32, bf16 = jnp.float32, jnp.bfloat16
    spaces, batches = lax.axis_size("space"), lax.axis_size("batch")
    owned_rows = np.arange(128).reshape(2, spaces, 4)
    to_slabs = owned_rows.transpose(1, 0, 2).reshape(-1)
    to_owner = np.argsort(to_slabs)
    up = [(i, i + 1) for i in range(spaces - 1)]
    down = [(i + 1, i) for i in range(spaces - 1)]
    local = volume[0]
    low = lax.ppermute(local[:, -1:], "space", up)
    high = lax.ppermute(local[:, :1], "space", down)
    sent = reorder(to_slabs, cotangent.reshape(128, 1024))
    cots = lax.all_to_all(sent, "space", split_axis=0, concat_axis=0, tiled=True)
    slab = jnp.pad(local, ((0, 0), (1, 1), (0, 0), (0, 0)))
    padded = jnp.pad(kernel, ((0, 0), (0, 128 - TAPS)))
    biases = jnp.broadcast_to(bias[:, None], (FILTERS, 128))
    pooled, window, code = in_vmem(
        forward_kernel,
        (
            jax.ShapeDtypeStruct((128, 1024), bf16),
            jax.ShapeDtypeStruct((256, 4096), bf16),
            jax.ShapeDtypeStruct((128, 1024), bf16),
        ),
        (slab, low, high, padded, biases),
        (
            pltpu.VMEM((1280, 128), f32),
            pltpu.VMEM((32, ROWS, 256), bf16),
            pltpu.VMEM((4, 8 * ROWS, 512), f32),
            pltpu.VMEM((128, 1024), bf16),
            pltpu.VMEM((256, 512), bf16),
        ),
        flops=1_000_000_000,
        moved=5_000_000,
    )
    out = in_vmem(
        backward_kernel,
        jax.ShapeDtypeStruct((128, 1152), bf16),
        (pooled, window, code, cots),
        (pltpu.VMEM((256, 4096), bf16), pltpu.VMEM((128, 1024), f32)),
        flops=600_000_000,
        moved=5_000_000,
    )

    out = lax.all_to_all(out, "space", split_axis=0, concat_axis=0, tiled=True)
    pooled = reorder(to_owner, out[:, :1024]).reshape(1, 2, 64, 1024)
    terms = jnp.sum(out[:, 1024:].reshape(spaces, 2, 4, 128).astype(f32), axis=(0, 2))
    terms = lax.all_to_all(
        jnp.broadcast_to(terms[None], (batches, 2, 128)), "batch", split_axis=0, concat_axis=0, tiled=True
    )
    terms = jnp.sum(terms, axis=0)
    terms = lax.all_to_all(
        jnp.broadcast_to(terms[None], (spaces, 2, 128)), "space", split_axis=0, concat_axis=0, tiled=True
    ).reshape(FILTERS, 128)
    kernel_grad, bias_grad = in_vmem(
        unpack_kernel,
        (jax.ShapeDtypeStruct((FILTERS, TAPS), f32), jax.ShapeDtypeStruct((1, FILTERS), f32)),
        (terms,),
        megabytes=4,
    )
    return (pooled, kernel_grad, bias_grad.reshape(FILTERS))


def solution(mesh):
    placed = (P("batch", None, "space", None, None), P(), P(), P("batch", "space", None, None))
    return jax.shard_map(
        on_device,
        mesh=mesh,
        in_specs=placed,
        out_specs=(P("batch", "space", None, None), P(), P()),
        check_vma=False,
    )
```

```python
import jax
import jax.numpy as jnp
import numpy as np
from jax import lax
from jax.experimental import pallas as pl
from jax.experimental.pallas import tpu as pltpu
from jax.sharding import PartitionSpec as P


CLASSES = [(pd, ph, pw) for pd in range(2) for ph in range(2) for pw in range(2)]
CHANNELS = 4
FILTERS = 32
TAPS = 27 * CHANNELS
ROWS = 48


def window_shift(pd, ph, pw):
    return ph * 64 + pw * 16 + pd * 4


def tap_table():
    tap = lax.broadcasted_iota(jnp.int32, (128, 256), 0)
    row = lax.broadcasted_iota(jnp.int32, (128, 256), 1)
    j, k, i, c = row >> 6, (row >> 4) & 3, (row >> 2) & 3, row & 3
    inside = (i < 3) & (j < 3) & (k < 3)
    return jnp.where(inside & (tap == (i * 9 + j * 3 + k) * CHANNELS + c), 1.0, 0.0).astype(jnp.bfloat16)


def width_table():
    row = lax.broadcasted_iota(jnp.int32, (256, 512), 0)
    col = lax.broadcasted_iota(jnp.int32, (256, 512), 1)
    same = (row >> 7) == ((col >> 6) & 1)
    return jnp.where(same & ((row & 127) == 2 * (col & 63) - 1 + (col >> 7)), 1.0, 0.0).astype(jnp.bfloat16)


def depth_table(inverse):
    row = lax.broadcasted_iota(jnp.int32, (128, 128), 0)
    col = lax.broadcasted_iota(jnp.int32, (128, 128), 1)
    if inverse:
        row, col = col, row
    return jnp.where(col == (row & 31) * 4 + (row >> 5), 1.0, 0.0).astype(jnp.bfloat16)


def row_table(order):
    table = np.zeros((128, 128), np.float32)
    table[np.arange(128), order] = 1.0
    return table


def reorder_kernel(rows_ref, last_ref, head_ref, out_ref):
    row = lax.broadcasted_iota(jnp.int32, (128, 128), 0)
    col = lax.broadcasted_iota(jnp.int32, (128, 128), 1)
    table = jnp.where(col == ((row >> 2) & 1) * 64 + (row >> 3) * 4 + (row & 3), 1.0, 0.0).astype(jnp.bfloat16)
    out_ref[...] = jnp.dot(table, rows_ref[...], preferred_element_type=jnp.float32).astype(jnp.bfloat16)


def inner_kernel(
    vol_ref, columns_ref, pooled_ref, window, code_ref, weights_ref, biases_ref,
    flat, lines, split, width, padded
):
    f32, bf16 = jnp.float32, jnp.bfloat16
    width[...] = width_table()
    padded[...] = jnp.zeros((FILTERS, 128), bf16)
    padded[:, :TAPS] = columns_ref[:, :TAPS].astype(bf16)
    spread_taps = jnp.dot(padded[...], tap_table(), preferred_element_type=f32)
    weights = jnp.concatenate(
        [
            pltpu.roll(spread_taps, window_shift(*parity), 1) if window_shift(*parity) else spread_taps
            for parity in CLASSES
        ],
        axis=0,
    ).astype(bf16)
    weights_ref[...] = weights
    bias = jnp.broadcast_to(columns_ref[:, TAPS : TAPS + 1], (FILTERS, 128))
    biases_ref[...] = bias

    flat[0:128, :] = jnp.zeros((128, 128), f32)
    flat[1152:1280, :] = jnp.zeros((128, 128), f32)
    for c in range(CHANNELS):
        for d in range(1, 9):
            flat[(d * CHANNELS + c) * 32 : (d * CHANNELS + c + 1) * 32, :] = vol_ref[c, d - 1].astype(f32)
    zero_line = jnp.zeros((ROWS, 128), bf16)
    lines[0, :, 0:128] = zero_line
    lines[31, :, 128:256] = zero_line
    for h in range(32):
        line = flat[pl.ds(h, 40, stride=32), :]
        line = jnp.concatenate([line, jnp.zeros((8, 128), f32)], axis=0).astype(bf16)
        if h <= 30:
            h4, j = divmod(h + 1, 4)
            lines[j * 8 + h4, :, 0:128] = line
        if h >= 1:
            h4, j = divmod(h - 1, 4)
            lines[j * 8 + h4, :, 128:256] = line
    for j in range(4):
        rows = lines[j * 8 : (j + 1) * 8].reshape(8 * ROWS, 256)
        split[j] = jnp.dot(rows, width[...], preferred_element_type=f32)
    for d2 in range(4):
        for h4 in range(8):
            for j in range(4):
                for k in range(4):
                    first = h4 * ROWS + d2 * 8
                    window[
                        (j * 4 + k) * 16 : (j * 4 + k + 1) * 16,
                        (d2 * 8 + h4) * 128 : (d2 * 8 + h4 + 1) * 128,
                    ] = split[j, first : first + 16, k * 128 : (k + 1) * 128].astype(bf16)

    for plane in range(2):
        rows = slice(plane * FILTERS, (plane + 1) * FILTERS)
        for tile in range(4):
            first = (plane + 1) * 1024 + tile * 256
            conv = jnp.dot(weights, window[:, first : first + 256], preferred_element_type=f32)
            for half in range(2):
                lane = tile * 256 + half * 128
                total = jnp.zeros((FILTERS, 128), f32)
                code = jnp.zeros((FILTERS, 128), f32)
                for n in range(8):
                    x = conv[n * FILTERS : (n + 1) * FILTERS, half * 128 : (half + 1) * 128] + bias
                    total = total + jnp.maximum(x, 0.3 * x).astype(bf16).astype(f32)
                    code = code + jnp.where(x > 0, float(1 << n), 0.0)
                code_ref[rows, lane : lane + 128] = code.astype(bf16)
                pooled_ref[rows, lane : lane + 128] = (total * 0.125).astype(bf16)


def outer_kernel(
    low_ref, high_ref, cot_ref, inner_ref, window, code_ref, weights_ref, biases_ref, out_ref,
    flat, lines, split, edge, spread, pooled, cots
):
    f32, bf16 = jnp.float32, jnp.bfloat16
    for c in range(CHANNELS):
        flat[c * 32 : (c + 1) * 32, :] = low_ref[c, 0].astype(f32)
        flat[(CHANNELS + c) * 32 : (CHANNELS + c + 1) * 32, :] = high_ref[c, 0].astype(f32)
    lines[0, :, 0:128] = jnp.zeros((8, 128), f32)
    lines[31, :, 128:256] = jnp.zeros((8, 128), f32)
    for h in range(32):
        line = flat[pl.ds(h, 8, stride=32), :]
        if h <= 30:
            h4, j = divmod(h + 1, 4)
            lines[j * 8 + h4, :, 0:128] = line
        if h >= 1:
            h4, j = divmod(h - 1, 4)
            lines[j * 8 + h4, :, 128:256] = line
    split[...] = jnp.dot(lines[...].reshape(256, 256).astype(bf16), width_table(), preferred_element_type=f32)

    cots[...] = jnp.dot(depth_table(False), cot_ref[...], preferred_element_type=f32)

    def gradients(d2, lane):
        incoming = cots[d2 * FILTERS : (d2 + 1) * FILTERS, lane : lane + 128] * 0.125
        return incoming.astype(bf16).astype(f32), (incoming * 0.3).astype(bf16).astype(f32)

    bias_sum = jnp.zeros((FILTERS, 128), f32)
    for plane in range(2):
        rows = slice((plane + 1) * FILTERS, (plane + 2) * FILTERS)
        held = slice(plane * FILTERS, (plane + 1) * FILTERS)
        pooled[rows, :] = inner_ref[held, :]
        for tile in range(8):
            lane = tile * 128
            first = (plane + 1) * 1024 + lane
            full, part = gradients(plane + 1, lane)
            code = code_ref[held, lane : lane + 128].astype(f32).astype(jnp.int32)
            for n in range(8):
                back = jnp.where((code & (1 << n)) != 0, full, part)
                bias_sum = bias_sum + back
                spread[n * FILTERS : (n + 1) * FILTERS, first : first + 128] = back.astype(bf16)
    grads = lax.dot_general(
        spread[:, 1024:3072], window[:, 1024:3072], (((1,), (1,)), ((), ())), preferred_element_type=f32
    )

    sublane = lax.broadcasted_iota(jnp.int32, (8, 128), 0)
    nothing = jnp.zeros((8, 128), f32)
    bias = biases_ref[...]
    for side in range(2):
        d2 = 3 * side
        for h4 in range(8):
            for j in range(4):
                for k in range(4):
                    rows = slice((j * 4 + k) * 16, (j * 4 + k + 1) * 16)
                    new = split[(j * 8 + h4) * 8 : (j * 8 + h4 + 1) * 8, k * 128 : (k + 1) * 128]
                    if side == 0:
                        new = jnp.concatenate([jnp.where(sublane < 4, new, 0.0), nothing], axis=0)
                    else:
                        new = jnp.concatenate([nothing, jnp.where(sublane < 4, 0.0, new)], axis=0)
                    own = window[rows, (d2 * 8 + h4) * 128 : (d2 * 8 + h4 + 1) * 128]
                    edge[rows, (side * 8 + h4) * 128 : (side * 8 + h4 + 1) * 128] = own + new.astype(bf16)
        for tile in range(4):
            first = side * 1024 + tile * 256
            conv = jnp.dot(weights_ref[...], edge[:, first : first + 256], preferred_element_type=f32)
            for half in range(2):
                lane = tile * 256 + half * 128
                full, part = gradients(d2, lane)
                total = jnp.zeros((FILTERS, 128), f32)
                for n in range(8):
                    x = conv[n * FILTERS : (n + 1) * FILTERS, half * 128 : (half + 1) * 128] + bias
                    total = total + jnp.maximum(x, 0.3 * x).astype(bf16).astype(f32)
                    back = jnp.where(x > 0, full, part)
                    bias_sum = bias_sum + back
                    spread[
                        n * FILTERS : (n + 1) * FILTERS, d2 * 1024 + lane : d2 * 1024 + lane + 128
                    ] = back.astype(bf16)
                pooled[d2 * FILTERS : (d2 + 1) * FILTERS, lane : lane + 128] = (total * 0.125).astype(bf16)
        grads = grads + lax.dot_general(
            spread[:, d2 * 1024 : (d2 + 1) * 1024],
            edge[:, side * 1024 : (side + 1) * 1024],
            (((1,), (1,)), ((), ())),
            preferred_element_type=f32,
        )
    out_ref[:, 0:1024] = jnp.dot(depth_table(True), pooled[...], preferred_element_type=f32).astype(bf16)

    table = tap_table()
    folded = jnp.zeros((FILTERS, 256), f32)
    for n, parity in enumerate(CLASSES):
        shift = window_shift(*parity)
        block = grads[n * FILTERS : (n + 1) * FILTERS]
        folded = folded + (pltpu.roll(block, 256 - shift, 1) if shift else block)

    def pieces(value):
        one = value.astype(bf16)
        rest = value - one.astype(f32)
        two = rest.astype(bf16)
        three = (rest - two.astype(f32)).astype(bf16)
        return one, two, three

    bias_column = jnp.sum(bias_sum, axis=1, keepdims=True)
    columns = lax.broadcasted_iota(jnp.int32, (FILTERS, 128), 1)
    sent = []
    for taps, own in zip(pieces(folded), pieces(bias_column), strict=True):
        picked = lax.dot_general(taps, table, (((1,), (1,)), ((), ())), preferred_element_type=f32)
        sent.append(jnp.where(columns == TAPS, own.astype(f32), picked))
    sent.append(jnp.zeros((FILTERS, 128), f32))
    stacked = jnp.concatenate(sent, axis=0).astype(bf16)
    out_ref[:, 1024:1152] = jnp.dot(depth_table(True), stacked, preferred_element_type=f32).astype(bf16)


def unpack_kernel(terms_ref, kernel_ref, bias_ref):
    terms = terms_ref[...]
    kernel_ref[...] = terms[:, :TAPS]
    own = lax.broadcasted_iota(jnp.int32, (FILTERS, FILTERS), 0) == lax.broadcasted_iota(
        jnp.int32, (FILTERS, FILTERS), 1
    )
    bias_ref[...] = jnp.sum(jnp.where(own, terms[:, TAPS : TAPS + 1], 0.0), axis=0, keepdims=True)


def in_vmem(kernel, outs, operands, scratch=(), megabytes=24, flops=1_000_000, moved=100_000):
    one = pl.BlockSpec(memory_space=pltpu.VMEM)
    return pl.pallas_call(
        kernel,
        out_shape=outs,
        in_specs=[one] * len(operands),
        out_specs=jax.tree.map(lambda _: one, outs),
        scratch_shapes=list(scratch),
        compiler_params=pltpu.CompilerParams(vmem_limit_bytes=megabytes * 1024 * 1024),
        cost_estimate=pl.CostEstimate(flops=flops, bytes_accessed=moved, transcendentals=0),
    )(*operands)


def reorder(order, rows):
    return jnp.dot(jnp.asarray(row_table(order), rows.dtype), rows, preferred_element_type=rows.dtype)


def on_device(volume, kernel, bias, cotangent):
    f32, bf16 = jnp.float32, jnp.bfloat16
    spaces, batches = lax.axis_size("space"), lax.axis_size("batch")
    owned_rows = np.arange(128).reshape(2, spaces, 4)
    to_slabs = owned_rows.transpose(1, 0, 2).reshape(-1)
    to_owner = np.argsort(to_slabs)
    up = [(i, i + 1) for i in range(spaces - 1)]
    down = [(i + 1, i) for i in range(spaces - 1)]
    local = volume[0]
    last, head = lax.optimization_barrier((local[:, -1:], local[:, :1]))
    sent = in_vmem(
        reorder_kernel,
        jax.ShapeDtypeStruct((128, 1024), bf16),
        (cotangent.reshape(128, 1024), last, head),
        megabytes=4,
    )
    cots = lax.all_to_all(sent, "space", split_axis=0, concat_axis=0, tiled=True)
    low = lax.ppermute(last, "space", up)
    high = lax.ppermute(head, "space", down)
    columns = jnp.concatenate([kernel.astype(f32), bias[:, None]], axis=1)
    shapes = (
        jax.ShapeDtypeStruct((64, 1024), bf16),
        jax.ShapeDtypeStruct((256, 4096), bf16),
        jax.ShapeDtypeStruct((64, 1024), bf16),
        jax.ShapeDtypeStruct((256, 256), bf16),
        jax.ShapeDtypeStruct((FILTERS, 128), f32),
    )
    inner = in_vmem(
        inner_kernel,
        shapes,
        (local, columns),
        (
            pltpu.VMEM((1280, 128), f32),
            pltpu.VMEM((32, ROWS, 256), bf16),
            pltpu.VMEM((4, 8 * ROWS, 512), f32),
            pltpu.VMEM((256, 512), bf16),
            pltpu.VMEM((FILTERS, 128), bf16),
        ),
        flops=1_000_000_000,
        moved=5_000_000,
    )
    out = in_vmem(
        outer_kernel,
        jax.ShapeDtypeStruct((128, 1152), bf16),
        (low, high, cots, *inner),
        (
            pltpu.VMEM((256, 128), f32),
            pltpu.VMEM((32, 8, 256), f32),
            pltpu.VMEM((256, 512), f32),
            pltpu.VMEM((256, 2048), bf16),
            pltpu.VMEM((256, 4096), bf16),
            pltpu.VMEM((128, 1024), bf16),
            pltpu.VMEM((128, 1024), f32),
        ),
        flops=600_000_000,
        moved=5_000_000,
    )

    out = lax.all_to_all(out, "space", split_axis=0, concat_axis=0, tiled=True)
    pooled = reorder(to_owner, out[:, :1024]).reshape(1, 2, 64, 1024)
    terms = jnp.sum(out[:, 1024:].reshape(spaces, 2, 4, 128).astype(f32), axis=(0, 2))
    terms = lax.all_to_all(
        jnp.broadcast_to(terms[None], (batches, 2, 128)), "batch", split_axis=0, concat_axis=0, tiled=True
    )
    terms = jnp.sum(terms, axis=0)
    terms = lax.all_to_all(
        jnp.broadcast_to(terms[None], (spaces, 2, 128)), "space", split_axis=0, concat_axis=0, tiled=True
    ).reshape(FILTERS, 128)
    kernel_grad, bias_grad = in_vmem(
        unpack_kernel,
        (jax.ShapeDtypeStruct((FILTERS, TAPS), f32), jax.ShapeDtypeStruct((1, FILTERS), f32)),
        (terms,),
        megabytes=4,
    )
    return (pooled, kernel_grad, bias_grad.reshape(FILTERS))


def solution(mesh):
    placed = (P("batch", None, "space", None, None), P(), P(), P("batch", "space", None, None))
    return jax.shard_map(
        on_device,
        mesh=mesh,
        in_specs=placed,
        out_specs=(P("batch", "space", None, None), P(), P()),
        check_vma=False,
    )
```

```python
import jax
import jax.numpy as jnp
import numpy as np
from jax import lax
from jax.experimental import pallas as pl
from jax.experimental.pallas import tpu as pltpu
from jax.sharding import PartitionSpec as P


CLASSES = [(pd, ph, pw) for pd in range(2) for ph in range(2) for pw in range(2)]
CHANNELS = 4
FILTERS = 32
TAPS = 27 * CHANNELS
ROWS = 48


def window_shift(pd, ph, pw):
    return ph * 64 + pw * 16 + pd * 4


def tap_table():
    tap = lax.broadcasted_iota(jnp.int32, (128, 256), 0)
    row = lax.broadcasted_iota(jnp.int32, (128, 256), 1)
    j, k, i, c = row >> 6, (row >> 4) & 3, (row >> 2) & 3, row & 3
    inside = (i < 3) & (j < 3) & (k < 3)
    return jnp.where(inside & (tap == (i * 9 + j * 3 + k) * CHANNELS + c), 1.0, 0.0).astype(jnp.bfloat16)


def width_table():
    row = lax.broadcasted_iota(jnp.int32, (256, 512), 0)
    col = lax.broadcasted_iota(jnp.int32, (256, 512), 1)
    same = (row >> 7) == ((col >> 6) & 1)
    return jnp.where(same & ((row & 127) == 2 * (col & 63) - 1 + (col >> 7)), 1.0, 0.0).astype(jnp.bfloat16)


def depth_table(inverse):
    row = lax.broadcasted_iota(jnp.int32, (128, 128), 0)
    col = lax.broadcasted_iota(jnp.int32, (128, 128), 1)
    if inverse:
        row, col = col, row
    return jnp.where(col == (row & 31) * 4 + (row >> 5), 1.0, 0.0).astype(jnp.bfloat16)


def row_table(order):
    table = np.zeros((128, 128), np.float32)
    table[np.arange(128), order] = 1.0
    return table


def reorder_kernel(rows_ref, last_ref, head_ref, out_ref):
    row = lax.broadcasted_iota(jnp.int32, (128, 128), 0)
    col = lax.broadcasted_iota(jnp.int32, (128, 128), 1)
    table = jnp.where(col == ((row >> 2) & 1) * 64 + (row >> 3) * 4 + (row & 3), 1.0, 0.0).astype(jnp.bfloat16)
    out_ref[...] = jnp.dot(table, rows_ref[...], preferred_element_type=jnp.float32).astype(jnp.bfloat16)


def inner_kernel(
    vol_ref, columns_ref, pooled_ref, window, code_ref, weights_ref, biases_ref,
    flat, lines, split, width, padded
):
    f32, bf16 = jnp.float32, jnp.bfloat16
    width[...] = width_table()
    padded[...] = jnp.zeros((FILTERS, 128), bf16)
    padded[:, :TAPS] = columns_ref[:, :TAPS].astype(bf16)
    spread_taps = jnp.dot(padded[...], tap_table(), preferred_element_type=f32)
    weights = jnp.concatenate(
        [
            pltpu.roll(spread_taps, window_shift(*parity), 1) if window_shift(*parity) else spread_taps
            for parity in CLASSES
        ],
        axis=0,
    ).astype(bf16)
    weights_ref[...] = weights
    bias = jnp.broadcast_to(columns_ref[:, TAPS : TAPS + 1], (FILTERS, 128))
    biases_ref[...] = bias

    flat[0:128, :] = jnp.zeros((128, 128), f32)
    flat[1152:1280, :] = jnp.zeros((128, 128), f32)
    for c in range(CHANNELS):
        for d in range(1, 9):
            flat[(d * CHANNELS + c) * 32 : (d * CHANNELS + c + 1) * 32, :] = vol_ref[c, d - 1].astype(f32)
    zero_line = jnp.zeros((ROWS, 128), bf16)
    lines[0, :, 0:128] = zero_line
    lines[31, :, 128:256] = zero_line
    for h in range(32):
        line = flat[pl.ds(h, 40, stride=32), :]
        line = jnp.concatenate([line, jnp.zeros((8, 128), f32)], axis=0).astype(bf16)
        if h <= 30:
            h4, j = divmod(h + 1, 4)
            lines[j * 8 + h4, :, 0:128] = line
        if h >= 1:
            h4, j = divmod(h - 1, 4)
            lines[j * 8 + h4, :, 128:256] = line
    for j in range(4):
        rows = lines[j * 8 : (j + 1) * 8].reshape(8 * ROWS, 256)
        split[j] = jnp.dot(rows, width[...], preferred_element_type=f32)
    for d2 in range(4):
        for h4 in range(8):
            for j in range(4):
                for k in range(4):
                    first = h4 * ROWS + d2 * 8
                    window[
                        (j * 4 + k) * 16 : (j * 4 + k + 1) * 16,
                        (d2 * 8 + h4) * 128 : (d2 * 8 + h4 + 1) * 128,
                    ] = split[j, first : first + 16, k * 128 : (k + 1) * 128].astype(bf16)

    for plane in range(2):
        rows = slice(plane * FILTERS, (plane + 1) * FILTERS)
        for tile in range(4):
            first = (plane + 1) * 1024 + tile * 256
            conv = jnp.dot(weights, window[:, first : first + 256], preferred_element_type=f32)
            for half in range(2):
                lane = tile * 256 + half * 128
                total = jnp.zeros((FILTERS, 128), f32)
                code = jnp.zeros((FILTERS, 128), f32)
                for n in range(8):
                    x = conv[n * FILTERS : (n + 1) * FILTERS, half * 128 : (half + 1) * 128] + bias
                    total = total + jnp.maximum(x, 0.3 * x).astype(bf16).astype(f32)
                    code = code + jnp.where(x > 0, float(1 << n), 0.0)
                code_ref[rows, lane : lane + 128] = code.astype(bf16)
                pooled_ref[rows, lane : lane + 128] = (total * 0.125).astype(bf16)


def outer_kernel(
    low_ref, high_ref, cot_ref, inner_ref, window, code_ref, weights_ref, biases_ref, out_ref,
    flat, lines, split, edge, spread, pooled, cots
):
    f32, bf16 = jnp.float32, jnp.bfloat16
    for c in range(CHANNELS):
        flat[c * 32 : (c + 1) * 32, :] = low_ref[c, 0].astype(f32)
        flat[(CHANNELS + c) * 32 : (CHANNELS + c + 1) * 32, :] = high_ref[c, 0].astype(f32)
    lines[0, :, 0:128] = jnp.zeros((8, 128), f32)
    lines[31, :, 128:256] = jnp.zeros((8, 128), f32)
    for h in range(32):
        line = flat[pl.ds(h, 8, stride=32), :]
        if h <= 30:
            h4, j = divmod(h + 1, 4)
            lines[j * 8 + h4, :, 0:128] = line
        if h >= 1:
            h4, j = divmod(h - 1, 4)
            lines[j * 8 + h4, :, 128:256] = line
    split[...] = jnp.dot(lines[...].reshape(256, 256).astype(bf16), width_table(), preferred_element_type=f32)

    cots[...] = jnp.dot(depth_table(False), cot_ref[...], preferred_element_type=f32)

    def gradients(d2, lane):
        incoming = cots[d2 * FILTERS : (d2 + 1) * FILTERS, lane : lane + 128] * 0.125
        return incoming.astype(bf16).astype(f32), (incoming * 0.3).astype(bf16).astype(f32)

    bias_sum = jnp.zeros((FILTERS, 128), f32)
    for plane in range(2):
        rows = slice((plane + 1) * FILTERS, (plane + 2) * FILTERS)
        held = slice(plane * FILTERS, (plane + 1) * FILTERS)
        pooled[rows, :] = inner_ref[held, :]
        for tile in range(8):
            lane = tile * 128
            first = (plane + 1) * 1024 + lane
            full, part = gradients(plane + 1, lane)
            code = code_ref[held, lane : lane + 128].astype(f32).astype(jnp.int32)
            for n in range(8):
                back = jnp.where((code & (1 << n)) != 0, full, part)
                bias_sum = bias_sum + back
                spread[n * FILTERS : (n + 1) * FILTERS, first : first + 128] = back.astype(bf16)
    grads = lax.dot_general(
        spread[:, 1024:3072], window[:, 1024:3072], (((1,), (1,)), ((), ())), preferred_element_type=f32
    )

    sublane = lax.broadcasted_iota(jnp.int32, (8, 128), 0)
    nothing = jnp.zeros((8, 128), f32)
    bias = biases_ref[...]
    for side in range(2):
        d2 = 3 * side
        for h4 in range(8):
            for j in range(4):
                for k in range(4):
                    rows = slice((j * 4 + k) * 16, (j * 4 + k + 1) * 16)
                    new = split[(j * 8 + h4) * 8 : (j * 8 + h4 + 1) * 8, k * 128 : (k + 1) * 128]
                    if side == 0:
                        new = jnp.concatenate([jnp.where(sublane < 4, new, 0.0), nothing], axis=0)
                    else:
                        new = jnp.concatenate([nothing, jnp.where(sublane < 4, 0.0, new)], axis=0)
                    own = window[rows, (d2 * 8 + h4) * 128 : (d2 * 8 + h4 + 1) * 128]
                    edge[rows, (side * 8 + h4) * 128 : (side * 8 + h4 + 1) * 128] = own + new.astype(bf16)
        for tile in range(4):
            first = side * 1024 + tile * 256
            conv = jnp.dot(weights_ref[...], edge[:, first : first + 256], preferred_element_type=f32)
            for half in range(2):
                lane = tile * 256 + half * 128
                full, part = gradients(d2, lane)
                total = jnp.zeros((FILTERS, 128), f32)
                for n in range(8):
                    x = conv[n * FILTERS : (n + 1) * FILTERS, half * 128 : (half + 1) * 128] + bias
                    total = total + jnp.maximum(x, 0.3 * x).astype(bf16).astype(f32)
                    back = jnp.where(x > 0, full, part)
                    bias_sum = bias_sum + back
                    spread[
                        n * FILTERS : (n + 1) * FILTERS, d2 * 1024 + lane : d2 * 1024 + lane + 128
                    ] = back.astype(bf16)
                pooled[d2 * FILTERS : (d2 + 1) * FILTERS, lane : lane + 128] = (total * 0.125).astype(bf16)
        grads = grads + lax.dot_general(
            spread[:, d2 * 1024 : (d2 + 1) * 1024],
            edge[:, side * 1024 : (side + 1) * 1024],
            (((1,), (1,)), ((), ())),
            preferred_element_type=f32,
        )
    out_ref[:, 0:1024] = jnp.dot(depth_table(True), pooled[...], preferred_element_type=f32).astype(bf16)

    table = tap_table()
    folded = jnp.zeros((FILTERS, 256), f32)
    for n, parity in enumerate(CLASSES):
        shift = window_shift(*parity)
        block = grads[n * FILTERS : (n + 1) * FILTERS]
        folded = folded + (pltpu.roll(block, 256 - shift, 1) if shift else block)

    def pieces(value):
        one = value.astype(bf16)
        rest = value - one.astype(f32)
        two = rest.astype(bf16)
        three = (rest - two.astype(f32)).astype(bf16)
        return one, two, three

    bias_column = jnp.sum(bias_sum, axis=1, keepdims=True)
    columns = lax.broadcasted_iota(jnp.int32, (FILTERS, 128), 1)
    sent = []
    for taps, own in zip(pieces(folded), pieces(bias_column), strict=True):
        picked = lax.dot_general(taps, table, (((1,), (1,)), ((), ())), preferred_element_type=f32)
        sent.append(jnp.where(columns == TAPS, own.astype(f32), picked))
    sent.append(jnp.zeros((FILTERS, 128), f32))
    stacked = jnp.concatenate(sent, axis=0).astype(bf16)
    out_ref[:, 1024:1152] = jnp.dot(depth_table(True), stacked, preferred_element_type=f32).astype(bf16)


def unpack_kernel(terms_ref, kernel_ref, bias_ref):
    terms = terms_ref[...]
    kernel_ref[...] = terms[:, :TAPS]
    own = lax.broadcasted_iota(jnp.int32, (FILTERS, FILTERS), 0) == lax.broadcasted_iota(
        jnp.int32, (FILTERS, FILTERS), 1
    )
    bias_ref[...] = jnp.sum(jnp.where(own, terms[:, TAPS : TAPS + 1], 0.0), axis=0, keepdims=True)


def in_vmem(kernel, outs, operands, scratch=(), megabytes=24, flops=1_000_000, moved=100_000):
    one = pl.BlockSpec(memory_space=pltpu.VMEM)
    return pl.pallas_call(
        kernel,
        out_shape=outs,
        in_specs=[one] * len(operands),
        out_specs=jax.tree.map(lambda _: one, outs),
        scratch_shapes=list(scratch),
        compiler_params=pltpu.CompilerParams(vmem_limit_bytes=megabytes * 1024 * 1024),
        cost_estimate=pl.CostEstimate(flops=flops, bytes_accessed=moved, transcendentals=0),
    )(*operands)


def reorder(order, rows):
    return jnp.dot(jnp.asarray(row_table(order), rows.dtype), rows, preferred_element_type=rows.dtype)


def on_device(volume, kernel, bias, cotangent):
    f32, bf16 = jnp.float32, jnp.bfloat16
    spaces, batches = lax.axis_size("space"), lax.axis_size("batch")
    owned_rows = np.arange(128).reshape(2, spaces, 4)
    to_slabs = owned_rows.transpose(1, 0, 2).reshape(-1)
    to_owner = np.argsort(to_slabs)
    up = [(i, i + 1) for i in range(spaces - 1)]
    down = [(i + 1, i) for i in range(spaces - 1)]
    local = volume[0]
    last, head = lax.optimization_barrier((local[:, -1:], local[:, :1]))
    sent = in_vmem(
        reorder_kernel,
        jax.ShapeDtypeStruct((128, 1024), bf16),
        (cotangent.reshape(128, 1024), last, head),
        megabytes=4,
    )
    cots = lax.all_to_all(sent, "space", split_axis=0, concat_axis=0, tiled=True)
    low = lax.ppermute(last, "space", up)
    high = lax.ppermute(head, "space", down)
    wide = jnp.pad(kernel, ((0, 0), (0, 128 - TAPS))).astype(f32)
    column = lax.broadcasted_iota(jnp.int32, (FILTERS, 128), 1)
    columns = jnp.where(column == TAPS, lax.broadcast_in_dim(bias, (FILTERS, 128), (0,)), wide)
    shapes = (
        jax.ShapeDtypeStruct((64, 1024), bf16),
        jax.ShapeDtypeStruct((256, 4096), bf16),
        jax.ShapeDtypeStruct((64, 1024), bf16),
        jax.ShapeDtypeStruct((256, 256), bf16),
        jax.ShapeDtypeStruct((FILTERS, 128), f32),
    )
    inner = in_vmem(
        inner_kernel,
        shapes,
        (local, columns),
        (
            pltpu.VMEM((1280, 128), f32),
            pltpu.VMEM((32, ROWS, 256), bf16),
            pltpu.VMEM((4, 8 * ROWS, 512), f32),
            pltpu.VMEM((256, 512), bf16),
            pltpu.VMEM((FILTERS, 128), bf16),
        ),
        flops=1_000_000_000,
        moved=5_000_000,
    )
    out = in_vmem(
        outer_kernel,
        jax.ShapeDtypeStruct((128, 1152), bf16),
        (low, high, cots, *inner),
        (
            pltpu.VMEM((256, 128), f32),
            pltpu.VMEM((32, 8, 256), f32),
            pltpu.VMEM((256, 512), f32),
            pltpu.VMEM((256, 2048), bf16),
            pltpu.VMEM((256, 4096), bf16),
            pltpu.VMEM((128, 1024), bf16),
            pltpu.VMEM((128, 1024), f32),
        ),
        flops=600_000_000,
        moved=5_000_000,
    )

    out = lax.all_to_all(out, "space", split_axis=0, concat_axis=0, tiled=True)
    pooled = reorder(to_owner, out[:, :1024]).reshape(1, 2, 64, 1024)
    terms = jnp.sum(out[:, 1024:].reshape(spaces, 2, 4, 128).astype(f32), axis=(0, 2))
    fine = 8
    coarse = batches // fine
    far = [[i + fine * k for k in range(coarse)] for i in range(fine)]
    near = [[fine * k + i for i in range(fine)] for k in range(coarse)]
    for groups in (far, near):
        copies = jnp.broadcast_to(terms[None], (len(groups[0]), 2, 128))
        terms = jnp.sum(
            lax.all_to_all(copies, "batch", split_axis=0, concat_axis=0, axis_index_groups=groups, tiled=True),
            axis=0,
        )
    terms = lax.all_to_all(
        jnp.broadcast_to(terms[None], (spaces, 2, 128)), "space", split_axis=0, concat_axis=0, tiled=True
    ).reshape(FILTERS, 128)
    kernel_grad, bias_grad = in_vmem(
        unpack_kernel,
        (jax.ShapeDtypeStruct((FILTERS, TAPS), f32), jax.ShapeDtypeStruct((1, FILTERS), f32)),
        (terms,),
        megabytes=4,
    )
    return (pooled, kernel_grad, bias_grad.reshape(FILTERS))


def solution(mesh):
    placed = (P("batch", None, "space", None, None), P(), P(), P("batch", "space", None, None))
    return jax.shard_map(
        on_device,
        mesh=mesh,
        in_specs=placed,
        out_specs=(P("batch", "space", None, None), P(), P()),
        check_vma=False,
    )
```

```python
import jax
import jax.numpy as jnp
import numpy as np
from jax import lax
from jax.experimental import pallas as pl
from jax.experimental.pallas import tpu as pltpu
from jax.sharding import PartitionSpec as P


CLASSES = [(pd, ph, pw) for pd in range(2) for ph in range(2) for pw in range(2)]
CHANNELS = 4
FILTERS = 32
TAPS = 27 * CHANNELS
ROWS = 48


def window_shift(pd, ph, pw):
    return ph * 64 + pw * 16 + pd * 4


def tap_table():
    tap = lax.broadcasted_iota(jnp.int32, (128, 256), 0)
    row = lax.broadcasted_iota(jnp.int32, (128, 256), 1)
    j, k, i, c = row >> 6, (row >> 4) & 3, (row >> 2) & 3, row & 3
    inside = (i < 3) & (j < 3) & (k < 3)
    return jnp.where(inside & (tap == (i * 9 + j * 3 + k) * CHANNELS + c), 1.0, 0.0).astype(jnp.bfloat16)


def width_table():
    row = lax.broadcasted_iota(jnp.int32, (256, 512), 0)
    col = lax.broadcasted_iota(jnp.int32, (256, 512), 1)
    same = (row >> 7) == ((col >> 6) & 1)
    return jnp.where(same & ((row & 127) == 2 * (col & 63) - 1 + (col >> 7)), 1.0, 0.0).astype(jnp.bfloat16)


def depth_table(inverse):
    row = lax.broadcasted_iota(jnp.int32, (128, 128), 0)
    col = lax.broadcasted_iota(jnp.int32, (128, 128), 1)
    if inverse:
        row, col = col, row
    return jnp.where(col == (row & 31) * 4 + (row >> 5), 1.0, 0.0).astype(jnp.bfloat16)


def row_table(order):
    table = np.zeros((128, 128), np.float32)
    table[np.arange(128), order] = 1.0
    return table


def reorder_kernel(rows_ref, out_ref):
    row = lax.broadcasted_iota(jnp.int32, (128, 128), 0)
    col = lax.broadcasted_iota(jnp.int32, (128, 128), 1)
    table = jnp.where(col == ((row >> 2) & 1) * 64 + (row >> 3) * 4 + (row & 3), 1.0, 0.0).astype(jnp.bfloat16)
    out_ref[...] = jnp.dot(table, rows_ref[...], preferred_element_type=jnp.float32).astype(jnp.bfloat16)


def inner_kernel(
    vol_ref, columns_ref, pooled_ref, window, code_ref, weights_ref, biases_ref,
    flat, lines, split, width, padded
):
    f32, bf16 = jnp.float32, jnp.bfloat16
    width[...] = width_table()
    padded[...] = jnp.zeros((FILTERS, 128), bf16)
    padded[:, :TAPS] = columns_ref[:, :TAPS].astype(bf16)
    spread_taps = jnp.dot(padded[...], tap_table(), preferred_element_type=f32)
    weights = jnp.concatenate(
        [
            pltpu.roll(spread_taps, window_shift(*parity), 1) if window_shift(*parity) else spread_taps
            for parity in CLASSES
        ],
        axis=0,
    ).astype(bf16)
    weights_ref[...] = weights
    bias = jnp.broadcast_to(columns_ref[:, TAPS : TAPS + 1], (FILTERS, 128))
    biases_ref[...] = bias

    for c in range(CHANNELS):
        for d in range(10):
            flat[(d * CHANNELS + c) * 32 : (d * CHANNELS + c + 1) * 32, :] = vol_ref[c, d].astype(f32)
    zero_line = jnp.zeros((ROWS, 128), bf16)
    lines[0, :, 0:128] = zero_line
    lines[31, :, 128:256] = zero_line
    for h in range(32):
        line = flat[pl.ds(h, 40, stride=32), :]
        line = jnp.concatenate([line, jnp.zeros((8, 128), f32)], axis=0).astype(bf16)
        if h <= 30:
            h4, j = divmod(h + 1, 4)
            lines[j * 8 + h4, :, 0:128] = line
        if h >= 1:
            h4, j = divmod(h - 1, 4)
            lines[j * 8 + h4, :, 128:256] = line
    for j in range(4):
        rows = lines[j * 8 : (j + 1) * 8].reshape(8 * ROWS, 256)
        split[j] = jnp.dot(rows, width[...], preferred_element_type=f32)
    for d2 in range(4):
        for h4 in range(8):
            for j in range(4):
                for k in range(4):
                    first = h4 * ROWS + d2 * 8
                    window[
                        (j * 4 + k) * 16 : (j * 4 + k + 1) * 16,
                        (d2 * 8 + h4) * 128 : (d2 * 8 + h4 + 1) * 128,
                    ] = split[j, first : first + 16, k * 128 : (k + 1) * 128].astype(bf16)

    for plane in range(2):
        rows = slice(plane * FILTERS, (plane + 1) * FILTERS)
        for tile in range(4):
            first = (plane + 1) * 1024 + tile * 256
            conv = jnp.dot(weights, window[:, first : first + 256], preferred_element_type=f32)
            for half in range(2):
                lane = tile * 256 + half * 128
                total = jnp.zeros((FILTERS, 128), f32)
                code = jnp.zeros((FILTERS, 128), f32)
                for n in range(8):
                    x = conv[n * FILTERS : (n + 1) * FILTERS, half * 128 : (half + 1) * 128] + bias
                    total = total + jnp.maximum(x, 0.3 * x).astype(bf16).astype(f32)
                    code = code + jnp.where(x > 0, float(1 << n), 0.0)
                code_ref[rows, lane : lane + 128] = code.astype(bf16)
                pooled_ref[rows, lane : lane + 128] = (total * 0.125).astype(bf16)


def outer_kernel(
    low_ref, high_ref, cot_ref, inner_ref, window, code_ref, weights_ref, biases_ref, out_ref,
    flat, lines, split, edge, spread, pooled, cots
):
    f32, bf16 = jnp.float32, jnp.bfloat16
    for c in range(CHANNELS):
        flat[c * 32 : (c + 1) * 32, :] = low_ref[c, 0].astype(f32)
        flat[(CHANNELS + c) * 32 : (CHANNELS + c + 1) * 32, :] = high_ref[c, 0].astype(f32)
    lines[0, :, 0:128] = jnp.zeros((8, 128), f32)
    lines[31, :, 128:256] = jnp.zeros((8, 128), f32)
    for h in range(32):
        line = flat[pl.ds(h, 8, stride=32), :]
        if h <= 30:
            h4, j = divmod(h + 1, 4)
            lines[j * 8 + h4, :, 0:128] = line
        if h >= 1:
            h4, j = divmod(h - 1, 4)
            lines[j * 8 + h4, :, 128:256] = line
    split[...] = jnp.dot(lines[...].reshape(256, 256).astype(bf16), width_table(), preferred_element_type=f32)

    cots[...] = jnp.dot(depth_table(False), cot_ref[...], preferred_element_type=f32)

    def gradients(d2, lane):
        incoming = cots[d2 * FILTERS : (d2 + 1) * FILTERS, lane : lane + 128] * 0.125
        return incoming.astype(bf16).astype(f32), (incoming * 0.3).astype(bf16).astype(f32)

    bias_sum = jnp.zeros((FILTERS, 128), f32)
    for plane in range(2):
        rows = slice((plane + 1) * FILTERS, (plane + 2) * FILTERS)
        held = slice(plane * FILTERS, (plane + 1) * FILTERS)
        pooled[rows, :] = inner_ref[held, :]
        for tile in range(8):
            lane = tile * 128
            first = (plane + 1) * 1024 + lane
            full, part = gradients(plane + 1, lane)
            code = code_ref[held, lane : lane + 128].astype(f32).astype(jnp.int32)
            for n in range(8):
                back = jnp.where((code & (1 << n)) != 0, full, part)
                bias_sum = bias_sum + back
                spread[n * FILTERS : (n + 1) * FILTERS, first : first + 128] = back.astype(bf16)
    grads = lax.dot_general(
        spread[:, 1024:3072], window[:, 1024:3072], (((1,), (1,)), ((), ())), preferred_element_type=f32
    )

    sublane = lax.broadcasted_iota(jnp.int32, (8, 128), 0)
    nothing = jnp.zeros((8, 128), f32)
    bias = biases_ref[...]
    for side in range(2):
        d2 = 3 * side
        for h4 in range(8):
            for j in range(4):
                for k in range(4):
                    rows = slice((j * 4 + k) * 16, (j * 4 + k + 1) * 16)
                    new = split[(j * 8 + h4) * 8 : (j * 8 + h4 + 1) * 8, k * 128 : (k + 1) * 128]
                    if side == 0:
                        new = jnp.concatenate([jnp.where(sublane < 4, new, 0.0), nothing], axis=0)
                    else:
                        new = jnp.concatenate([nothing, jnp.where(sublane < 4, 0.0, new)], axis=0)
                    own = window[rows, (d2 * 8 + h4) * 128 : (d2 * 8 + h4 + 1) * 128]
                    edge[rows, (side * 8 + h4) * 128 : (side * 8 + h4 + 1) * 128] = own + new.astype(bf16)
        for tile in range(4):
            first = side * 1024 + tile * 256
            conv = jnp.dot(weights_ref[...], edge[:, first : first + 256], preferred_element_type=f32)
            for half in range(2):
                lane = tile * 256 + half * 128
                full, part = gradients(d2, lane)
                total = jnp.zeros((FILTERS, 128), f32)
                for n in range(8):
                    x = conv[n * FILTERS : (n + 1) * FILTERS, half * 128 : (half + 1) * 128] + bias
                    total = total + jnp.maximum(x, 0.3 * x).astype(bf16).astype(f32)
                    back = jnp.where(x > 0, full, part)
                    bias_sum = bias_sum + back
                    spread[
                        n * FILTERS : (n + 1) * FILTERS, d2 * 1024 + lane : d2 * 1024 + lane + 128
                    ] = back.astype(bf16)
                pooled[d2 * FILTERS : (d2 + 1) * FILTERS, lane : lane + 128] = (total * 0.125).astype(bf16)
        grads = grads + lax.dot_general(
            spread[:, d2 * 1024 : (d2 + 1) * 1024],
            edge[:, side * 1024 : (side + 1) * 1024],
            (((1,), (1,)), ((), ())),
            preferred_element_type=f32,
        )
    out_ref[:, 0:1024] = jnp.dot(depth_table(True), pooled[...], preferred_element_type=f32).astype(bf16)

    table = tap_table()
    folded = jnp.zeros((FILTERS, 256), f32)
    for n, parity in enumerate(CLASSES):
        shift = window_shift(*parity)
        block = grads[n * FILTERS : (n + 1) * FILTERS]
        folded = folded + (pltpu.roll(block, 256 - shift, 1) if shift else block)

    def pieces(value):
        one = value.astype(bf16)
        rest = value - one.astype(f32)
        two = rest.astype(bf16)
        three = (rest - two.astype(f32)).astype(bf16)
        return one, two, three

    bias_column = jnp.sum(bias_sum, axis=1, keepdims=True)
    columns = lax.broadcasted_iota(jnp.int32, (FILTERS, 128), 1)
    sent = []
    for taps, own in zip(pieces(folded), pieces(bias_column), strict=True):
        picked = lax.dot_general(taps, table, (((1,), (1,)), ((), ())), preferred_element_type=f32)
        sent.append(jnp.where(columns == TAPS, own.astype(f32), picked))
    sent.append(jnp.zeros((FILTERS, 128), f32))
    stacked = jnp.concatenate(sent, axis=0).astype(bf16)
    out_ref[:, 1024:1152] = jnp.dot(depth_table(True), stacked, preferred_element_type=f32).astype(bf16)


def unpack_kernel(terms_ref, kernel_ref, bias_ref):
    terms = terms_ref[...]
    kernel_ref[...] = terms[:, :TAPS]
    own = lax.broadcasted_iota(jnp.int32, (FILTERS, FILTERS), 0) == lax.broadcasted_iota(
        jnp.int32, (FILTERS, FILTERS), 1
    )
    bias_ref[...] = jnp.sum(jnp.where(own, terms[:, TAPS : TAPS + 1], 0.0), axis=0, keepdims=True)


def in_vmem(kernel, outs, operands, scratch=(), megabytes=24, flops=1_000_000, moved=100_000):
    one = pl.BlockSpec(memory_space=pltpu.VMEM)
    return pl.pallas_call(
        kernel,
        out_shape=outs,
        in_specs=[one] * len(operands),
        out_specs=jax.tree.map(lambda _: one, outs),
        scratch_shapes=list(scratch),
        compiler_params=pltpu.CompilerParams(vmem_limit_bytes=megabytes * 1024 * 1024),
        cost_estimate=pl.CostEstimate(flops=flops, bytes_accessed=moved, transcendentals=0),
    )(*operands)


def reorder(order, rows):
    return jnp.dot(jnp.asarray(row_table(order), rows.dtype), rows, preferred_element_type=rows.dtype)


def on_device(volume, kernel, bias, cotangent):
    f32, bf16 = jnp.float32, jnp.bfloat16
    spaces, batches = lax.axis_size("space"), lax.axis_size("batch")
    owned_rows = np.arange(128).reshape(2, spaces, 4)
    to_slabs = owned_rows.transpose(1, 0, 2).reshape(-1)
    to_owner = np.argsort(to_slabs)
    up = [(i, i + 1) for i in range(spaces - 1)]
    down = [(i + 1, i) for i in range(spaces - 1)]
    local = volume[0]
    slab = lax.optimization_barrier(jnp.pad(local, ((0, 0), (1, 1), (0, 0), (0, 0))))
    last, head = slab[:, -2:-1], slab[:, 1:2]
    sent = in_vmem(
        reorder_kernel,
        jax.ShapeDtypeStruct((128, 1024), bf16),
        (cotangent.reshape(128, 1024),),
        megabytes=4,
    )
    cots = lax.all_to_all(sent, "space", split_axis=0, concat_axis=0, tiled=True)
    low = lax.ppermute(last, "space", up)
    high = lax.ppermute(head, "space", down)
    wide = jnp.pad(kernel, ((0, 0), (0, 128 - TAPS))).astype(f32)
    column = lax.broadcasted_iota(jnp.int32, (FILTERS, 128), 1)
    columns = jnp.where(column == TAPS, lax.broadcast_in_dim(bias, (FILTERS, 128), (0,)), wide)
    shapes = (
        jax.ShapeDtypeStruct((64, 1024), bf16),
        jax.ShapeDtypeStruct((256, 4096), bf16),
        jax.ShapeDtypeStruct((64, 1024), bf16),
        jax.ShapeDtypeStruct((256, 256), bf16),
        jax.ShapeDtypeStruct((FILTERS, 128), f32),
    )
    inner = in_vmem(
        inner_kernel,
        shapes,
        (slab, columns),
        (
            pltpu.VMEM((1280, 128), f32),
            pltpu.VMEM((32, ROWS, 256), bf16),
            pltpu.VMEM((4, 8 * ROWS, 512), f32),
            pltpu.VMEM((256, 512), bf16),
            pltpu.VMEM((FILTERS, 128), bf16),
        ),
        flops=1_000_000_000,
        moved=5_000_000,
    )
    out = in_vmem(
        outer_kernel,
        jax.ShapeDtypeStruct((128, 1152), bf16),
        (low, high, cots, *inner),
        (
            pltpu.VMEM((256, 128), f32),
            pltpu.VMEM((32, 8, 256), f32),
            pltpu.VMEM((256, 512), f32),
            pltpu.VMEM((256, 2048), bf16),
            pltpu.VMEM((256, 4096), bf16),
            pltpu.VMEM((128, 1024), bf16),
            pltpu.VMEM((128, 1024), f32),
        ),
        flops=600_000_000,
        moved=5_000_000,
    )

    out = lax.all_to_all(out, "space", split_axis=0, concat_axis=0, tiled=True)
    pooled = reorder(to_owner, out[:, :1024]).reshape(1, 2, 64, 1024)
    terms = jnp.sum(out[:, 1024:].reshape(spaces, 2, 4, 128).astype(f32), axis=(0, 2))
    other = [(i, i ^ 1) for i in range(batches)]
    cores = [list(range(core, batches, 2)) for core in range(2)]
    terms = terms + lax.ppermute(terms, "batch", other)
    copies = jnp.broadcast_to(terms[None], (batches // 2, 2, 128))
    terms = jnp.sum(
        lax.all_to_all(copies, "batch", split_axis=0, concat_axis=0, axis_index_groups=cores, tiled=True), axis=0
    )
    terms = lax.all_to_all(
        jnp.broadcast_to(terms[None], (spaces, 2, 128)), "space", split_axis=0, concat_axis=0, tiled=True
    ).reshape(FILTERS, 128)
    kernel_grad, bias_grad = in_vmem(
        unpack_kernel,
        (jax.ShapeDtypeStruct((FILTERS, TAPS), f32), jax.ShapeDtypeStruct((1, FILTERS), f32)),
        (terms,),
        megabytes=4,
    )
    return (pooled, kernel_grad, bias_grad.reshape(FILTERS))


def solution(mesh):
    placed = (P("batch", None, "space", None, None), P(), P(), P("batch", "space", None, None))
    return jax.shard_map(
        on_device,
        mesh=mesh,
        in_specs=placed,
        out_specs=(P("batch", "space", None, None), P(), P()),
        check_vma=False,
    )
```

```python
import jax
import jax.numpy as jnp
import numpy as np
from jax import lax
from jax.experimental import pallas as pl
from jax.experimental.pallas import tpu as pltpu
from jax.sharding import PartitionSpec as P


CLASSES = [(pd, ph, pw) for pd in range(2) for ph in range(2) for pw in range(2)]
CHANNELS = 4
FILTERS = 32
TAPS = 27 * CHANNELS
ROWS = 48


def window_shift(pd, ph, pw):
    return ph * 64 + pw * 16 + pd * 4


def tap_table():
    tap = lax.broadcasted_iota(jnp.int32, (128, 256), 0)
    row = lax.broadcasted_iota(jnp.int32, (128, 256), 1)
    j, k, i, c = row >> 6, (row >> 4) & 3, (row >> 2) & 3, row & 3
    inside = (i < 3) & (j < 3) & (k < 3)
    return jnp.where(inside & (tap == (i * 9 + j * 3 + k) * CHANNELS + c), 1.0, 0.0).astype(jnp.bfloat16)


def width_table():
    row = lax.broadcasted_iota(jnp.int32, (256, 512), 0)
    col = lax.broadcasted_iota(jnp.int32, (256, 512), 1)
    same = (row >> 7) == ((col >> 6) & 1)
    return jnp.where(same & ((row & 127) == 2 * (col & 63) - 1 + (col >> 7)), 1.0, 0.0).astype(jnp.bfloat16)


def depth_table(inverse):
    row = lax.broadcasted_iota(jnp.int32, (128, 128), 0)
    col = lax.broadcasted_iota(jnp.int32, (128, 128), 1)
    if inverse:
        row, col = col, row
    return jnp.where(col == (row & 31) * 4 + (row >> 5), 1.0, 0.0).astype(jnp.bfloat16)


def row_table(order):
    table = np.zeros((128, 128), np.float32)
    table[np.arange(128), order] = 1.0
    return table


def reorder_kernel(rows_ref, out_ref):
    row = lax.broadcasted_iota(jnp.int32, (128, 128), 0)
    col = lax.broadcasted_iota(jnp.int32, (128, 128), 1)
    table = jnp.where(col == ((row >> 2) & 1) * 64 + (row >> 3) * 4 + (row & 3), 1.0, 0.0).astype(jnp.bfloat16)
    out_ref[...] = jnp.dot(table, rows_ref[...], preferred_element_type=jnp.float32).astype(jnp.bfloat16)


def inner_kernel(
    vol_ref, columns_ref, pooled_ref, window, code_ref, weights_ref, biases_ref,
    flat, lines, split, width, padded
):
    f32, bf16 = jnp.float32, jnp.bfloat16
    width[...] = width_table()
    padded[...] = jnp.zeros((FILTERS, 128), bf16)
    padded[:, :TAPS] = columns_ref[:, :TAPS].astype(bf16)
    spread_taps = jnp.dot(padded[...], tap_table(), preferred_element_type=f32)
    weights = jnp.concatenate(
        [
            pltpu.roll(spread_taps, window_shift(*parity), 1) if window_shift(*parity) else spread_taps
            for parity in CLASSES
        ],
        axis=0,
    ).astype(bf16)
    weights_ref[...] = weights
    bias = jnp.broadcast_to(columns_ref[:, TAPS : TAPS + 1], (FILTERS, 128))
    biases_ref[...] = bias

    for c in range(CHANNELS):
        for d in range(10):
            flat[(d * CHANNELS + c) * 32 : (d * CHANNELS + c + 1) * 32, :] = vol_ref[c, d].astype(f32)
    zero_line = jnp.zeros((ROWS, 128), bf16)
    lines[0, :, 0:128] = zero_line
    lines[31, :, 128:256] = zero_line
    for h in range(32):
        line = flat[pl.ds(h, 40, stride=32), :]
        line = jnp.concatenate([line, jnp.zeros((8, 128), f32)], axis=0).astype(bf16)
        if h <= 30:
            h4, j = divmod(h + 1, 4)
            lines[j * 8 + h4, :, 0:128] = line
        if h >= 1:
            h4, j = divmod(h - 1, 4)
            lines[j * 8 + h4, :, 128:256] = line
    for j in range(4):
        rows = lines[j * 8 : (j + 1) * 8].reshape(8 * ROWS, 256)
        split[j] = jnp.dot(rows, width[...], preferred_element_type=f32)
    for d2 in range(4):
        for h4 in range(8):
            for j in range(4):
                for k in range(4):
                    first = h4 * ROWS + d2 * 8
                    window[
                        (j * 4 + k) * 16 : (j * 4 + k + 1) * 16,
                        (d2 * 8 + h4) * 128 : (d2 * 8 + h4 + 1) * 128,
                    ] = split[j, first : first + 16, k * 128 : (k + 1) * 128].astype(bf16)

    for plane in range(2):
        rows = slice(plane * FILTERS, (plane + 1) * FILTERS)
        for tile in range(4):
            first = (plane + 1) * 1024 + tile * 256
            conv = jnp.dot(weights, window[:, first : first + 256], preferred_element_type=f32)
            for half in range(2):
                lane = tile * 256 + half * 128
                total = jnp.zeros((FILTERS, 128), f32)
                code = jnp.zeros((FILTERS, 128), f32)
                for n in range(8):
                    x = conv[n * FILTERS : (n + 1) * FILTERS, half * 128 : (half + 1) * 128] + bias
                    total = total + jnp.maximum(x, 0.3 * x).astype(bf16).astype(f32)
                    code = code + jnp.where(x > 0, float(1 << n), 0.0)
                code_ref[rows, lane : lane + 128] = code.astype(bf16)
                pooled_ref[rows, lane : lane + 128] = (total * 0.125).astype(bf16)


def gradients(cots, d2, lane):
    f32, bf16 = jnp.float32, jnp.bfloat16
    incoming = cots[d2 * FILTERS : (d2 + 1) * FILTERS, lane : lane + 128].astype(f32) * 0.125
    return incoming.astype(bf16).astype(f32), (incoming * 0.3).astype(bf16).astype(f32)


def middle_kernel(cot_ref, window, code_ref, cots, grads_ref, sums_ref, spread):
    f32, bf16 = jnp.float32, jnp.bfloat16
    cots[...] = jnp.dot(depth_table(False), cot_ref[...], preferred_element_type=f32).astype(bf16)
    bias_sum = jnp.zeros((FILTERS, 128), f32)
    for plane in range(2):
        held = slice(plane * FILTERS, (plane + 1) * FILTERS)
        for tile in range(8):
            lane = tile * 128
            first = plane * 1024 + lane
            full, part = gradients(cots, plane + 1, lane)
            code = code_ref[held, lane : lane + 128].astype(f32).astype(jnp.int32)
            for n in range(8):
                back = jnp.where((code & (1 << n)) != 0, full, part)
                bias_sum = bias_sum + back
                spread[n * FILTERS : (n + 1) * FILTERS, first : first + 128] = back.astype(bf16)
    grads_ref[...] = lax.dot_general(
        spread[...], window[:, 1024:3072], (((1,), (1,)), ((), ())), preferred_element_type=f32
    )
    sums_ref[...] = bias_sum


def outer_kernel(
    low_ref, high_ref, weights_ref, biases_ref, inner_ref, window, cots, grads_ref, sums_ref, out_ref,
    flat, lines, split, edge, spread, pooled
):
    f32, bf16 = jnp.float32, jnp.bfloat16
    for c in range(CHANNELS):
        flat[c * 32 : (c + 1) * 32, :] = low_ref[c, 0].astype(f32)
        flat[(CHANNELS + c) * 32 : (CHANNELS + c + 1) * 32, :] = high_ref[c, 0].astype(f32)
    lines[0, :, 0:128] = jnp.zeros((8, 128), f32)
    lines[31, :, 128:256] = jnp.zeros((8, 128), f32)
    for h in range(32):
        line = flat[pl.ds(h, 8, stride=32), :]
        if h <= 30:
            h4, j = divmod(h + 1, 4)
            lines[j * 8 + h4, :, 0:128] = line
        if h >= 1:
            h4, j = divmod(h - 1, 4)
            lines[j * 8 + h4, :, 128:256] = line
    split[...] = jnp.dot(lines[...].reshape(256, 256).astype(bf16), width_table(), preferred_element_type=f32)

    pooled[FILTERS : 3 * FILTERS, :] = inner_ref[...]
    bias_sum, grads = sums_ref[...], grads_ref[...]

    sublane = lax.broadcasted_iota(jnp.int32, (8, 128), 0)
    nothing = jnp.zeros((8, 128), f32)
    bias = biases_ref[...]
    for side in range(2):
        d2 = 3 * side
        for h4 in range(8):
            for j in range(4):
                for k in range(4):
                    rows = slice((j * 4 + k) * 16, (j * 4 + k + 1) * 16)
                    new = split[(j * 8 + h4) * 8 : (j * 8 + h4 + 1) * 8, k * 128 : (k + 1) * 128]
                    if side == 0:
                        new = jnp.concatenate([jnp.where(sublane < 4, new, 0.0), nothing], axis=0)
                    else:
                        new = jnp.concatenate([nothing, jnp.where(sublane < 4, 0.0, new)], axis=0)
                    own = window[rows, (d2 * 8 + h4) * 128 : (d2 * 8 + h4 + 1) * 128]
                    edge[rows, (side * 8 + h4) * 128 : (side * 8 + h4 + 1) * 128] = own + new.astype(bf16)
        for tile in range(4):
            first = side * 1024 + tile * 256
            conv = jnp.dot(weights_ref[...], edge[:, first : first + 256], preferred_element_type=f32)
            for half in range(2):
                lane = tile * 256 + half * 128
                full, part = gradients(cots, d2, lane)
                total = jnp.zeros((FILTERS, 128), f32)
                for n in range(8):
                    x = conv[n * FILTERS : (n + 1) * FILTERS, half * 128 : (half + 1) * 128] + bias
                    total = total + jnp.maximum(x, 0.3 * x).astype(bf16).astype(f32)
                    back = jnp.where(x > 0, full, part)
                    bias_sum = bias_sum + back
                    spread[
                        n * FILTERS : (n + 1) * FILTERS, side * 1024 + lane : side * 1024 + lane + 128
                    ] = back.astype(bf16)
                pooled[d2 * FILTERS : (d2 + 1) * FILTERS, lane : lane + 128] = (total * 0.125).astype(bf16)
        grads = grads + lax.dot_general(
            spread[:, side * 1024 : (side + 1) * 1024],
            edge[:, side * 1024 : (side + 1) * 1024],
            (((1,), (1,)), ((), ())),
            preferred_element_type=f32,
        )
    out_ref[:, 0:1024] = jnp.dot(depth_table(True), pooled[...], preferred_element_type=f32).astype(bf16)

    table = tap_table()
    folded = jnp.zeros((FILTERS, 256), f32)
    for n, parity in enumerate(CLASSES):
        shift = window_shift(*parity)
        block = grads[n * FILTERS : (n + 1) * FILTERS]
        folded = folded + (pltpu.roll(block, 256 - shift, 1) if shift else block)

    def pieces(value):
        one = value.astype(bf16)
        rest = value - one.astype(f32)
        two = rest.astype(bf16)
        three = (rest - two.astype(f32)).astype(bf16)
        return one, two, three

    bias_column = jnp.sum(bias_sum, axis=1, keepdims=True)
    columns = lax.broadcasted_iota(jnp.int32, (FILTERS, 128), 1)
    sent = []
    for taps, own in zip(pieces(folded), pieces(bias_column), strict=True):
        picked = lax.dot_general(taps, table, (((1,), (1,)), ((), ())), preferred_element_type=f32)
        sent.append(jnp.where(columns == TAPS, own.astype(f32), picked))
    sent.append(jnp.zeros((FILTERS, 128), f32))
    stacked = jnp.concatenate(sent, axis=0).astype(bf16)
    out_ref[:, 1024:1152] = jnp.dot(depth_table(True), stacked, preferred_element_type=f32).astype(bf16)


def unpack_kernel(terms_ref, kernel_ref, bias_ref):
    terms = terms_ref[...]
    kernel_ref[...] = terms[:, :TAPS]
    own = lax.broadcasted_iota(jnp.int32, (FILTERS, FILTERS), 0) == lax.broadcasted_iota(
        jnp.int32, (FILTERS, FILTERS), 1
    )
    bias_ref[...] = jnp.sum(jnp.where(own, terms[:, TAPS : TAPS + 1], 0.0), axis=0, keepdims=True)


def in_vmem(kernel, outs, operands, scratch=(), megabytes=24, flops=1_000_000, moved=100_000):
    one = pl.BlockSpec(memory_space=pltpu.VMEM)
    return pl.pallas_call(
        kernel,
        out_shape=outs,
        in_specs=[one] * len(operands),
        out_specs=jax.tree.map(lambda _: one, outs),
        scratch_shapes=list(scratch),
        compiler_params=pltpu.CompilerParams(vmem_limit_bytes=megabytes * 1024 * 1024),
        cost_estimate=pl.CostEstimate(flops=flops, bytes_accessed=moved, transcendentals=0),
    )(*operands)


def reorder(order, rows):
    return jnp.dot(jnp.asarray(row_table(order), rows.dtype), rows, preferred_element_type=rows.dtype)


def on_device(volume, kernel, bias, cotangent):
    f32, bf16 = jnp.float32, jnp.bfloat16
    spaces, batches = lax.axis_size("space"), lax.axis_size("batch")
    owned_rows = np.arange(128).reshape(2, spaces, 4)
    to_slabs = owned_rows.transpose(1, 0, 2).reshape(-1)
    to_owner = np.argsort(to_slabs)
    up = [(i, i + 1) for i in range(spaces - 1)]
    down = [(i + 1, i) for i in range(spaces - 1)]
    local = volume[0]
    slab = lax.optimization_barrier(jnp.pad(local, ((0, 0), (1, 1), (0, 0), (0, 0))))
    last, head = slab[:, -2:-1], slab[:, 1:2]
    sent = in_vmem(
        reorder_kernel,
        jax.ShapeDtypeStruct((128, 1024), bf16),
        (cotangent.reshape(128, 1024),),
        megabytes=4,
    )
    cots = lax.all_to_all(sent, "space", split_axis=0, concat_axis=0, tiled=True)
    low = lax.ppermute(last, "space", up)
    high = lax.ppermute(head, "space", down)
    wide = jnp.pad(kernel, ((0, 0), (0, 128 - TAPS))).astype(f32)
    column = lax.broadcasted_iota(jnp.int32, (FILTERS, 128), 1)
    columns = jnp.where(column == TAPS, lax.broadcast_in_dim(bias, (FILTERS, 128), (0,)), wide)
    shapes = (
        jax.ShapeDtypeStruct((64, 1024), bf16),
        jax.ShapeDtypeStruct((256, 4096), bf16),
        jax.ShapeDtypeStruct((64, 1024), bf16),
        jax.ShapeDtypeStruct((256, 256), bf16),
        jax.ShapeDtypeStruct((FILTERS, 128), f32),
    )
    inner = in_vmem(
        inner_kernel,
        shapes,
        (slab, columns),
        (
            pltpu.VMEM((1280, 128), f32),
            pltpu.VMEM((32, ROWS, 256), bf16),
            pltpu.VMEM((4, 8 * ROWS, 512), f32),
            pltpu.VMEM((256, 512), bf16),
            pltpu.VMEM((FILTERS, 128), bf16),
        ),
        flops=1_000_000_000,
        moved=5_000_000,
    )
    pooled, window, code, weights, biases = inner
    cots, grads, sums = in_vmem(
        middle_kernel,
        (
            jax.ShapeDtypeStruct((128, 1024), bf16),
            jax.ShapeDtypeStruct((256, 256), f32),
            jax.ShapeDtypeStruct((FILTERS, 128), f32),
        ),
        (cots, window, code),
        (pltpu.VMEM((256, 2048), bf16),),
        flops=300_000_000,
        moved=3_000_000,
    )
    out = in_vmem(
        outer_kernel,
        jax.ShapeDtypeStruct((128, 1152), bf16),
        (low, high, weights, biases, pooled, window, cots, grads, sums),
        (
            pltpu.VMEM((256, 128), f32),
            pltpu.VMEM((32, 8, 256), f32),
            pltpu.VMEM((256, 512), f32),
            pltpu.VMEM((256, 2048), bf16),
            pltpu.VMEM((256, 2048), bf16),
            pltpu.VMEM((128, 1024), bf16),
        ),
        flops=400_000_000,
        moved=4_000_000,
    )

    out = lax.all_to_all(out, "space", split_axis=0, concat_axis=0, tiled=True)
    pooled = reorder(to_owner, out[:, :1024]).reshape(1, 2, 64, 1024)
    terms = jnp.sum(out[:, 1024:].reshape(spaces, 2, 4, 128).astype(f32), axis=(0, 2))
    terms = lax.all_to_all(
        jnp.broadcast_to(terms[None], (batches, 2, 128)), "batch", split_axis=0, concat_axis=0, tiled=True
    )
    terms = jnp.sum(terms, axis=0)
    terms = lax.all_to_all(
        jnp.broadcast_to(terms[None], (spaces, 2, 128)), "space", split_axis=0, concat_axis=0, tiled=True
    ).reshape(FILTERS, 128)
    kernel_grad, bias_grad = in_vmem(
        unpack_kernel,
        (jax.ShapeDtypeStruct((FILTERS, TAPS), f32), jax.ShapeDtypeStruct((1, FILTERS), f32)),
        (terms,),
        megabytes=4,
    )
    return (pooled, kernel_grad, bias_grad.reshape(FILTERS))


def solution(mesh):
    placed = (P("batch", None, "space", None, None), P(), P(), P("batch", "space", None, None))
    return jax.shard_map(
        on_device,
        mesh=mesh,
        in_specs=placed,
        out_specs=(P("batch", "space", None, None), P(), P()),
        check_vma=False,
    )
```

```python
import jax
import jax.numpy as jnp
import numpy as np
from jax import lax
from jax.experimental import pallas as pl
from jax.experimental.pallas import tpu as pltpu
from jax.sharding import PartitionSpec as P


CLASSES = [(pd, ph, pw) for pd in range(2) for ph in range(2) for pw in range(2)]
CHANNELS = 4
FILTERS = 32
TAPS = 27 * CHANNELS
ROWS = 48


def window_shift(pd, ph, pw):
    return ph * 64 + pw * 16 + pd * 4


def tap_table():
    tap = lax.broadcasted_iota(jnp.int32, (128, 256), 0)
    row = lax.broadcasted_iota(jnp.int32, (128, 256), 1)
    j, k, i, c = row >> 6, (row >> 4) & 3, (row >> 2) & 3, row & 3
    inside = (i < 3) & (j < 3) & (k < 3)
    return jnp.where(inside & (tap == (i * 9 + j * 3 + k) * CHANNELS + c), 1.0, 0.0).astype(jnp.bfloat16)


def width_table():
    row = lax.broadcasted_iota(jnp.int32, (256, 512), 0)
    col = lax.broadcasted_iota(jnp.int32, (256, 512), 1)
    same = (row >> 7) == ((col >> 6) & 1)
    return jnp.where(same & ((row & 127) == 2 * (col & 63) - 1 + (col >> 7)), 1.0, 0.0).astype(jnp.bfloat16)


def depth_table(inverse):
    row = lax.broadcasted_iota(jnp.int32, (128, 128), 0)
    col = lax.broadcasted_iota(jnp.int32, (128, 128), 1)
    if inverse:
        row, col = col, row
    return jnp.where(col == (row & 31) * 4 + (row >> 5), 1.0, 0.0).astype(jnp.bfloat16)


def row_table(order):
    table = np.zeros((128, 128), np.float32)
    table[np.arange(128), order] = 1.0
    return table


def reorder_kernel(rows_ref, out_ref):
    row = lax.broadcasted_iota(jnp.int32, (128, 128), 0)
    col = lax.broadcasted_iota(jnp.int32, (128, 128), 1)
    table = jnp.where(col == ((row >> 2) & 1) * 64 + (row >> 3) * 4 + (row & 3), 1.0, 0.0).astype(jnp.bfloat16)
    out_ref[...] = jnp.dot(table, rows_ref[...], preferred_element_type=jnp.float32).astype(jnp.bfloat16)


def inner_kernel(
    vol_ref, columns_ref, pooled_ref, window, code_ref, weights_ref, biases_ref,
    flat, lines, split, width, padded
):
    f32, bf16 = jnp.float32, jnp.bfloat16
    width[...] = width_table()
    padded[...] = jnp.zeros((FILTERS, 128), bf16)
    padded[:, :TAPS] = columns_ref[:, :TAPS].astype(bf16)
    spread_taps = jnp.dot(padded[...], tap_table(), preferred_element_type=f32)
    weights = jnp.concatenate(
        [
            pltpu.roll(spread_taps, window_shift(*parity), 1) if window_shift(*parity) else spread_taps
            for parity in CLASSES
        ],
        axis=0,
    ).astype(bf16)
    weights_ref[...] = weights
    bias = jnp.broadcast_to(columns_ref[:, TAPS : TAPS + 1], (FILTERS, 128))
    biases_ref[...] = bias

    for c in range(CHANNELS):
        for d in range(10):
            flat[(d * CHANNELS + c) * 32 : (d * CHANNELS + c + 1) * 32, :] = vol_ref[c, d].astype(f32)
    zero_line = jnp.zeros((ROWS, 128), bf16)
    lines[0, :, 0:128] = zero_line
    lines[31, :, 128:256] = zero_line
    for h in range(32):
        line = flat[pl.ds(h, 40, stride=32), :]
        line = jnp.concatenate([line, jnp.zeros((8, 128), f32)], axis=0).astype(bf16)
        if h <= 30:
            h4, j = divmod(h + 1, 4)
            lines[j * 8 + h4, :, 0:128] = line
        if h >= 1:
            h4, j = divmod(h - 1, 4)
            lines[j * 8 + h4, :, 128:256] = line
    for j in range(4):
        rows = lines[j * 8 : (j + 1) * 8].reshape(8 * ROWS, 256)
        split[j] = jnp.dot(rows, width[...], preferred_element_type=f32)
    for d2 in range(4):
        for h4 in range(8):
            for j in range(4):
                for k in range(4):
                    first = h4 * ROWS + d2 * 8
                    window[
                        (j * 4 + k) * 16 : (j * 4 + k + 1) * 16,
                        (d2 * 8 + h4) * 128 : (d2 * 8 + h4 + 1) * 128,
                    ] = split[j, first : first + 16, k * 128 : (k + 1) * 128].astype(bf16)

    for plane in range(2):
        rows = slice(plane * FILTERS, (plane + 1) * FILTERS)
        for tile in range(4):
            first = (plane + 1) * 1024 + tile * 256
            conv = jnp.dot(weights, window[:, first : first + 256], preferred_element_type=f32)
            for half in range(2):
                lane = tile * 256 + half * 128
                total = jnp.zeros((FILTERS, 128), f32)
                code = jnp.zeros((FILTERS, 128), f32)
                for n in range(8):
                    x = conv[n * FILTERS : (n + 1) * FILTERS, half * 128 : (half + 1) * 128] + bias
                    total = total + jnp.maximum(x, 0.3 * x).astype(bf16).astype(f32)
                    code = code + jnp.where(x > 0, float(1 << n), 0.0)
                code_ref[rows, lane : lane + 128] = code.astype(bf16)
                pooled_ref[rows, lane : lane + 128] = (total * 0.125).astype(bf16)


def gradients(cots, d2, lane):
    f32, bf16 = jnp.float32, jnp.bfloat16
    incoming = cots[d2 * FILTERS : (d2 + 1) * FILTERS, lane : lane + 128].astype(f32) * 0.125
    return incoming.astype(bf16).astype(f32), (incoming * 0.3).astype(bf16).astype(f32)


def middle_kernel(cot_ref, window, code_ref, cots, grads_ref, sums_ref, spread):
    f32, bf16 = jnp.float32, jnp.bfloat16
    cots[...] = jnp.dot(depth_table(False), cot_ref[...], preferred_element_type=f32).astype(bf16)
    bias_sum = jnp.zeros((FILTERS, 128), f32)
    for plane in range(2):
        held = slice(plane * FILTERS, (plane + 1) * FILTERS)
        for tile in range(8):
            lane = tile * 128
            first = plane * 1024 + lane
            full, part = gradients(cots, plane + 1, lane)
            code = code_ref[held, lane : lane + 128].astype(f32).astype(jnp.int32)
            for n in range(8):
                back = jnp.where((code & (1 << n)) != 0, full, part)
                bias_sum = bias_sum + back
                spread[n * FILTERS : (n + 1) * FILTERS, first : first + 128] = back.astype(bf16)
    grads_ref[...] = lax.dot_general(
        spread[...], window[:, 1024:3072], (((1,), (1,)), ((), ())), preferred_element_type=f32
    )
    sums_ref[...] = bias_sum


def outer_kernel(
    low_ref, high_ref, weights_ref, biases_ref, inner_ref, window, cots, grads_ref, sums_ref, out_ref,
    flat, lines, split, edge, spread, pooled
):
    f32, bf16 = jnp.float32, jnp.bfloat16
    for c in range(CHANNELS):
        flat[c * 32 : (c + 1) * 32, :] = low_ref[c, 0].astype(f32)
        flat[(CHANNELS + c) * 32 : (CHANNELS + c + 1) * 32, :] = high_ref[c, 0].astype(f32)
    lines[0, :, 0:128] = jnp.zeros((8, 128), f32)
    lines[31, :, 128:256] = jnp.zeros((8, 128), f32)
    for h in range(32):
        line = flat[pl.ds(h, 8, stride=32), :]
        if h <= 30:
            h4, j = divmod(h + 1, 4)
            lines[j * 8 + h4, :, 0:128] = line
        if h >= 1:
            h4, j = divmod(h - 1, 4)
            lines[j * 8 + h4, :, 128:256] = line
    split[...] = jnp.dot(lines[...].reshape(256, 256).astype(bf16), width_table(), preferred_element_type=f32)

    pooled[FILTERS : 3 * FILTERS, :] = inner_ref[...]
    bias_sum, grads = sums_ref[...], grads_ref[...]

    sublane = lax.broadcasted_iota(jnp.int32, (8, 128), 0)
    nothing = jnp.zeros((8, 128), f32)
    bias = biases_ref[...]
    for side in range(2):
        d2 = 3 * side
        for h4 in range(8):
            for j in range(4):
                for k in range(4):
                    rows = slice((j * 4 + k) * 16, (j * 4 + k + 1) * 16)
                    new = split[(j * 8 + h4) * 8 : (j * 8 + h4 + 1) * 8, k * 128 : (k + 1) * 128]
                    if side == 0:
                        new = jnp.concatenate([jnp.where(sublane < 4, new, 0.0), nothing], axis=0)
                    else:
                        new = jnp.concatenate([nothing, jnp.where(sublane < 4, 0.0, new)], axis=0)
                    own = window[rows, (d2 * 8 + h4) * 128 : (d2 * 8 + h4 + 1) * 128]
                    edge[rows, (side * 8 + h4) * 128 : (side * 8 + h4 + 1) * 128] = own + new.astype(bf16)
        for tile in range(4):
            first = side * 1024 + tile * 256
            conv = jnp.dot(weights_ref[...], edge[:, first : first + 256], preferred_element_type=f32)
            for half in range(2):
                lane = tile * 256 + half * 128
                full, part = gradients(cots, d2, lane)
                total = jnp.zeros((FILTERS, 128), f32)
                for n in range(8):
                    x = conv[n * FILTERS : (n + 1) * FILTERS, half * 128 : (half + 1) * 128] + bias
                    total = total + jnp.maximum(x, 0.3 * x).astype(bf16).astype(f32)
                    back = jnp.where(x > 0, full, part)
                    bias_sum = bias_sum + back
                    spread[
                        n * FILTERS : (n + 1) * FILTERS, side * 1024 + lane : side * 1024 + lane + 128
                    ] = back.astype(bf16)
                pooled[d2 * FILTERS : (d2 + 1) * FILTERS, lane : lane + 128] = (total * 0.125).astype(bf16)
        grads = grads + lax.dot_general(
            spread[:, side * 1024 : (side + 1) * 1024],
            edge[:, side * 1024 : (side + 1) * 1024],
            (((1,), (1,)), ((), ())),
            preferred_element_type=f32,
        )
    out_ref[:, 0:1024] = jnp.dot(depth_table(True), pooled[...], preferred_element_type=f32).astype(bf16)

    table = tap_table()
    folded = jnp.zeros((FILTERS, 256), f32)
    for n, parity in enumerate(CLASSES):
        shift = window_shift(*parity)
        block = grads[n * FILTERS : (n + 1) * FILTERS]
        folded = folded + (pltpu.roll(block, 256 - shift, 1) if shift else block)

    def pieces(value):
        one = value.astype(bf16)
        rest = value - one.astype(f32)
        two = rest.astype(bf16)
        three = (rest - two.astype(f32)).astype(bf16)
        return one, two, three

    bias_column = jnp.sum(bias_sum, axis=1, keepdims=True)
    columns = lax.broadcasted_iota(jnp.int32, (FILTERS, 128), 1)
    sent = []
    for taps, own in zip(pieces(folded), pieces(bias_column), strict=True):
        picked = lax.dot_general(taps, table, (((1,), (1,)), ((), ())), preferred_element_type=f32)
        sent.append(jnp.where(columns == TAPS, own.astype(f32), picked))
    sent.append(jnp.zeros((FILTERS, 128), f32))
    stacked = jnp.concatenate(sent, axis=0).astype(bf16)
    out_ref[:, 1024:1152] = jnp.dot(depth_table(True), stacked, preferred_element_type=f32).astype(bf16)


def share_kernel(parts_ref, copies_ref):
    total = jnp.sum(parts_ref[...], axis=0)
    copies_ref[...] = jnp.broadcast_to(total[None], copies_ref.shape)


def unpack_kernel(terms_ref, kernel_ref, bias_ref):
    terms = terms_ref[...]
    kernel_ref[...] = terms[:, :TAPS]
    own = lax.broadcasted_iota(jnp.int32, (FILTERS, FILTERS), 0) == lax.broadcasted_iota(
        jnp.int32, (FILTERS, FILTERS), 1
    )
    bias_ref[...] = jnp.sum(jnp.where(own, terms[:, TAPS : TAPS + 1], 0.0), axis=0, keepdims=True)


def in_vmem(kernel, outs, operands, scratch=(), megabytes=24, flops=1_000_000, moved=100_000):
    one = pl.BlockSpec(memory_space=pltpu.VMEM)
    return pl.pallas_call(
        kernel,
        out_shape=outs,
        in_specs=[one] * len(operands),
        out_specs=jax.tree.map(lambda _: one, outs),
        scratch_shapes=list(scratch),
        compiler_params=pltpu.CompilerParams(vmem_limit_bytes=megabytes * 1024 * 1024),
        cost_estimate=pl.CostEstimate(flops=flops, bytes_accessed=moved, transcendentals=0),
    )(*operands)


def reorder(order, rows):
    return jnp.dot(jnp.asarray(row_table(order), rows.dtype), rows, preferred_element_type=rows.dtype)


def on_device(volume, kernel, bias, cotangent):
    f32, bf16 = jnp.float32, jnp.bfloat16
    spaces, batches = lax.axis_size("space"), lax.axis_size("batch")
    owned_rows = np.arange(128).reshape(2, spaces, 4)
    to_slabs = owned_rows.transpose(1, 0, 2).reshape(-1)
    to_owner = np.argsort(to_slabs)
    up = [(i, i + 1) for i in range(spaces - 1)]
    down = [(i + 1, i) for i in range(spaces - 1)]
    local = volume[0]
    slab = lax.optimization_barrier(jnp.pad(local, ((0, 0), (1, 1), (0, 0), (0, 0))))
    last, head = slab[:, -2:-1], slab[:, 1:2]
    sent = in_vmem(
        reorder_kernel,
        jax.ShapeDtypeStruct((128, 1024), bf16),
        (cotangent.reshape(128, 1024),),
        megabytes=4,
    )
    cots = lax.all_to_all(sent, "space", split_axis=0, concat_axis=0, tiled=True)
    low = lax.ppermute(last, "space", up)
    high = lax.ppermute(head, "space", down)
    wide = jnp.pad(kernel, ((0, 0), (0, 128 - TAPS))).astype(f32)
    column = lax.broadcasted_iota(jnp.int32, (FILTERS, 128), 1)
    columns = jnp.where(column == TAPS, lax.broadcast_in_dim(bias, (FILTERS, 128), (0,)), wide)
    shapes = (
        jax.ShapeDtypeStruct((64, 1024), bf16),
        jax.ShapeDtypeStruct((256, 4096), bf16),
        jax.ShapeDtypeStruct((64, 1024), bf16),
        jax.ShapeDtypeStruct((256, 256), bf16),
        jax.ShapeDtypeStruct((FILTERS, 128), f32),
    )
    inner = in_vmem(
        inner_kernel,
        shapes,
        (slab, columns),
        (
            pltpu.VMEM((1280, 128), f32),
            pltpu.VMEM((32, ROWS, 256), bf16),
            pltpu.VMEM((4, 8 * ROWS, 512), f32),
            pltpu.VMEM((256, 512), bf16),
            pltpu.VMEM((FILTERS, 128), bf16),
        ),
        flops=1_000_000_000,
        moved=5_000_000,
    )
    pooled, window, code, weights, biases = inner
    cots, grads, sums = in_vmem(
        middle_kernel,
        (
            jax.ShapeDtypeStruct((128, 1024), bf16),
            jax.ShapeDtypeStruct((256, 256), f32),
            jax.ShapeDtypeStruct((FILTERS, 128), f32),
        ),
        (cots, window, code),
        (pltpu.VMEM((256, 2048), bf16),),
        flops=300_000_000,
        moved=3_000_000,
    )
    out = in_vmem(
        outer_kernel,
        jax.ShapeDtypeStruct((128, 1152), bf16),
        (low, high, weights, biases, pooled, window, cots, grads, sums),
        (
            pltpu.VMEM((256, 128), f32),
            pltpu.VMEM((32, 8, 256), f32),
            pltpu.VMEM((256, 512), f32),
            pltpu.VMEM((256, 2048), bf16),
            pltpu.VMEM((256, 2048), bf16),
            pltpu.VMEM((128, 1024), bf16),
        ),
        flops=400_000_000,
        moved=4_000_000,
    )

    out = lax.all_to_all(out, "space", split_axis=0, concat_axis=0, tiled=True)
    pooled = reorder(to_owner, out[:, :1024]).reshape(1, 2, 64, 1024)
    terms = jnp.sum(out[:, 1024:].reshape(spaces, 2, 4, 128).astype(f32), axis=(0, 2))
    terms = lax.all_to_all(
        jnp.broadcast_to(terms[None], (batches, 2, 128)), "batch", split_axis=0, concat_axis=0, tiled=True
    )
    copies = in_vmem(share_kernel, jax.ShapeDtypeStruct((spaces, 2, 128), f32), (terms,), megabytes=4)
    terms = lax.all_to_all(copies, "space", split_axis=0, concat_axis=0, tiled=True).reshape(FILTERS, 128)
    kernel_grad, bias_grad = in_vmem(
        unpack_kernel,
        (jax.ShapeDtypeStruct((FILTERS, TAPS), f32), jax.ShapeDtypeStruct((1, FILTERS), f32)),
        (terms,),
        megabytes=4,
    )
    return (pooled, kernel_grad, bias_grad.reshape(FILTERS))


def solution(mesh):
    placed = (P("batch", None, "space", None, None), P(), P(), P("batch", "space", None, None))
    return jax.shard_map(
        on_device,
        mesh=mesh,
        in_specs=placed,
        out_specs=(P("batch", "space", None, None), P(), P()),
        check_vma=False,
    )
```
